32 devices in a mesh: cube: 2 (over x), chain: 16 (over z, y, core).
Axes of the slice: x: 2, y: 2, z: 4, core: 2. Of those that a mesh axis runs over, the one named last changes fastest.
Arguments:
- conserved: bfloat16 [2, 16, 5, 64, 1024], P('cube', 'chain'), may hold values from -1 to 6, as said below
- element_counts: int32 [2, 16], P('cube', 'chain'), may hold values from 512 to 1024, as said below
- face_links: int32 [2, 16, 4, 1024], P('cube', 'chain'), may hold values from 0 to 1023, as said below
- refinement: int32 [2, 16, 1024], P('cube', 'chain'), may hold values from 0 to 3
- derivative: bfloat16 [3, 64, 64], replicated, may hold values from -0.75 to 0.75
- face_lift: bfloat16 [64, 64], replicated, may hold values from -0.75 to 0.75
Outputs:
- balanced: bfloat16 [2, 16, 5, 64, 1024], P('cube', 'chain')
- balanced_levels: int32 [2, 16, 1024], P('cube', 'chain')
The draws below stay inside these ranges and needn't reach their ends.
Inputs may be any that keep to these rules, and one draw needn't show every extreme that they name: `element_counts`: along cube, every chain index has one device with exactly 1024 live elements and another with exactly 512; live elements fill the slots below the count. `face_links`: each entry names a live slot of the neighbouring device of that face. `conserved`: every node holds a physical state: density and pressure between 0.5 and 2, each velocity component between -0.5 and 0.5.
All inputs are finite; a program needn't handle non-finite values.
Results may differ from the reference program's by a relative error of at most 0.0026.
Values may be sent and summed in bfloat16 or wider, within the bound.
A program may use at most 64 MiB of HBM per device.

```python
import math
import jax
import jax.numpy as jnp
from jax import lax

NODES = 64
FNODES = 16
HOP = 4
SLOTS = 1024
ROUNDS = 1
N_CUBE = 2
N_CHAIN = 16


HEAT_RATIO = 1.4


def load_draw(key):
    folded = jax.random.fold_in(key, 7)
    first_key, second_key, third_key = jax.random.split(folded, 3)
    baseline = jax.random.randint(first_key, (N_CUBE, N_CHAIN), SLOTS // 2, SLOTS // 2 + SLOTS // 8 + 1)
    fullest = jax.random.randint(second_key, (N_CHAIN,), 0, N_CUBE)
    offset = jax.random.randint(third_key, (N_CHAIN,), 1, N_CUBE)
    lightest = (fullest + offset) % N_CUBE
    cube_rows = jnp.arange(N_CUBE, dtype=jnp.int32)[:, None]
    baseline = jnp.where(cube_rows == fullest[None, :], SLOTS, baseline)
    baseline = jnp.where(cube_rows == lightest[None, :], SLOTS // 2, baseline)
    return baseline.astype(jnp.int32)


def draw_element_counts(key, part):
    return load_draw(key)


def draw_face_links(key, part):
    loads = load_draw(key)
    neighbour_loads = jnp.stack([jnp.roll(loads, 1, axis=1), jnp.roll(loads, -1, axis=1), jnp.roll(loads, HOP, axis=1), jnp.roll(loads, -HOP, axis=1)], axis=2)
    random_slot = jax.random.randint(jax.random.fold_in(key, 13), (N_CUBE, N_CHAIN, 4, SLOTS), 0, 1 << 24)
    return (random_slot % neighbour_loads[..., None]).astype(jnp.int32)


def draw_conserved(key, part):
    grid_shape = (N_CUBE, N_CHAIN, NODES, SLOTS)
    subkeys = jax.random.split(jax.random.fold_in(key, 29), 3)
    density = jnp.exp(jax.random.uniform(subkeys[0], grid_shape, jnp.float32, math.log(0.5), math.log(2.0)))
    velocity = jnp.clip(0.2 * jax.random.normal(subkeys[1], (3,) + grid_shape, jnp.float32), -0.5, 0.5)
    pressure = jnp.exp(jax.random.uniform(subkeys[2], grid_shape, jnp.float32, math.log(0.5), math.log(2.0)))
    momenta = density[None] * velocity
    kinetic = velocity[0] * velocity[0] + velocity[1] * velocity[1] + velocity[2] * velocity[2]
    energy = pressure / (HEAT_RATIO - 1.0) + 0.5 * density * kinetic
    fields = jnp.concatenate([density[None], momenta, energy[None]], axis=0)
    return jnp.moveaxis(fields, 0, 2).astype(jnp.bfloat16)


def place_ends(values, key, low, top_value):
    extent = values.shape
    place = [jax.random.randint(jax.random.fold_in(key, axis), (), 0, extent[axis]) for axis in range(len(extent))]
    values = values.at[tuple(place)].set(low)
    longest = extent.index(max(extent))
    place[longest] = (place[longest] + 1) % extent[longest]
    return values.at[tuple(place)].set(top_value)


def gaussian(stream_key, dims, scale, reach, held_as=jnp.bfloat16):
    array = jax.random.normal(stream_key, dims, jnp.float32) * scale
    return jnp.minimum(jnp.maximum(array, -reach), reach).astype(held_as)


def setup_inputs(seed: int = 0) -> dict:
    seeds = jax.random.split(jax.random.key(seed), 7)
    conserved = draw_conserved(jax.random.fold_in(seeds[6], 71), 0)
    element_counts = draw_element_counts(jax.random.fold_in(seeds[6], 71), 0)
    face_links = draw_face_links(jax.random.fold_in(seeds[6], 71), 0)
    refinement = place_ends(jax.random.randint(seeds[3], (N_CUBE, N_CHAIN, SLOTS), 0, 4), jax.random.fold_in(seeds[3], 1), 0, 3).astype(jnp.int32)
    derivative = gaussian(seeds[4], (3, NODES, NODES), NODES ** -0.5, 0.75)
    face_lift = gaussian(seeds[5], (NODES, 4 * FNODES), (4 * FNODES) ** -0.5, 0.75)
    return {"conserved": conserved, "element_counts": element_counts, "face_links": face_links, "refinement": refinement, "derivative": derivative, "face_lift": face_lift}


HEAT_RATIO = 1.4
TIME_STEP = 0.08
FACE_AXES = (2, 2, 1, 1)
FACE_SIGNS = (-1.0, 1.0, -1.0, 1.0)

def flux_along(fields, axis_id):
    density = fields[0]
    momenta = fields[1:4]
    energy = fields[4]
    velocity = momenta[axis_id] / density
    kinetic = momenta[0] * momenta[0] + momenta[1] * momenta[1] + momenta[2] * momenta[2]
    pressure = (HEAT_RATIO - 1.0) * (energy - 0.5 * kinetic / density)
    pieces = [momenta[axis_id]]
    for column in range(3):
        component = momenta[column] * velocity
        if column == axis_id:
            component = component + pressure
        pieces.append(component)
    pieces.append((energy + pressure) * velocity)
    return (jnp.stack(pieces), velocity, pressure)

def face_jump(inner, neighbour, axis_id, orient):
    inner_flux, inner_vel, inner_press = flux_along(inner, axis_id)
    outer_flux, outer_vel, outer_press = flux_along(neighbour, axis_id)
    wave_speed = jnp.maximum(jnp.abs(inner_vel) + jnp.sqrt(HEAT_RATIO * inner_press / inner[0]), jnp.abs(outer_vel) + jnp.sqrt(HEAT_RATIO * outer_press / neighbour[0]))
    return 0.5 * orient * (inner_flux - outer_flux) + 0.5 * wave_speed * (neighbour - inner)

def face_traces(element_block):
    fields_count = element_block.shape[0]
    slot_count = element_block.shape[-1]
    cubed = element_block.reshape(fields_count, 4, 4, 4, slot_count)
    lower_z = cubed[:, 0].reshape(fields_count, 16, slot_count)
    upper_z = cubed[:, 3].reshape(fields_count, 16, slot_count)
    lower_y = cubed[:, :, 0].reshape(fields_count, 16, slot_count)
    upper_y = cubed[:, :, 3].reshape(fields_count, 16, slot_count)
    return (lower_z, upper_z, lower_y, upper_y)

def section_block(element_block, neighbours, level_row, derivative, face_lift):
    inner = element_block.astype(jnp.float32)
    fluxes = jnp.stack([flux_along(inner, axis_id)[0] for axis_id in range(3)]).astype(jnp.bfloat16)
    volume = jnp.einsum('dab,dfbs->fas', derivative.astype(jnp.float32), fluxes.astype(jnp.float32))
    own_faces = face_traces(inner)
    jumps = jnp.concatenate([face_jump(own_faces[face_id], neighbours[face_id].astype(jnp.float32), FACE_AXES[face_id], FACE_SIGNS[face_id]) for face_id in range(4)], axis=1).astype(jnp.bfloat16)
    surface = jnp.einsum('ab,fbs->fas', face_lift.astype(jnp.float32), jumps.astype(jnp.float32))
    factor = (jnp.int32(1) << level_row).astype(jnp.float32)
    return (inner + TIME_STEP * factor * (surface - volume)).astype(jnp.bfloat16)

def rebalance(blocks, loads):
    cube_count = blocks.shape[0]
    slot_count = blocks.shape[-1]
    middle = (1,) * (blocks.ndim - 2)
    position = jnp.arange(slot_count, dtype=jnp.int32)
    members = jnp.arange(cube_count, dtype=jnp.int32)
    for exponent in range(ROUNDS):
        partners = members ^ 1 << exponent
        partner_loads = loads[partners]
        leaving = jnp.maximum(loads - partner_loads, 0) // 2
        arriving = leaving[partners]
        staying = loads - leaving
        source = position[None, :] - staying[:, None] + partner_loads[:, None] - arriving[:, None]
        source = jnp.clip(source, 0, slot_count - 1)
        picks = jnp.broadcast_to(source.reshape((cube_count,) + middle + (slot_count,)), blocks.shape)
        fetched = jnp.take_along_axis(blocks[partners], picks, axis=blocks.ndim - 1)
        kept = (position[None, :] < staying[:, None]).reshape((cube_count,) + middle + (slot_count,))
        window = (position[None, :] < (staying + arriving)[:, None]).reshape((cube_count,) + middle + (slot_count,))
        blocks = jnp.where(kept, blocks, jnp.where(window, fetched, jnp.zeros_like(blocks)))
        loads = staying + arriving
    return blocks

def reference(conserved, element_counts, face_links, refinement, derivative, face_lift):
    cube_count, chain_count, fields_count, node_count, slot_count = conserved.shape
    cubed = conserved.reshape(cube_count, chain_count, fields_count, 4, 4, 4, slot_count)
    lower_z = cubed[:, :, :, 0].reshape(cube_count, chain_count, fields_count, 16, slot_count)
    upper_z = cubed[:, :, :, 3].reshape(cube_count, chain_count, fields_count, 16, slot_count)
    lower_y = cubed[:, :, :, :, 0].reshape(cube_count, chain_count, fields_count, 16, slot_count)
    upper_y = cubed[:, :, :, :, 3].reshape(cube_count, chain_count, fields_count, 16, slot_count)
    sources = (upper_z, lower_z, upper_y, lower_y)
    offsets = (-1, 1, -HOP, HOP)

    def column(chain_at):
        blocks = lax.dynamic_index_in_dim(conserved, chain_at, 1, keepdims=False)
        links_here = lax.dynamic_index_in_dim(face_links, chain_at, 1, keepdims=False)
        neighbours = []
        for face_id in range(4):
            other_chain = (chain_at + offsets[face_id]) % chain_count
            block_faces = lax.dynamic_index_in_dim(sources[face_id], other_chain, 1, keepdims=False)
            picks = jnp.broadcast_to(links_here[:, face_id][:, None, None, :], block_faces.shape)
            neighbours.append(jnp.take_along_axis(block_faces, picks, axis=3))
        level_here = lax.dynamic_index_in_dim(refinement, chain_at, 1, keepdims=False)
        sectioned = jax.vmap(section_block, in_axes=(0, 0, 0, None, None))(blocks, tuple(neighbours), level_here, derivative, face_lift)
        loads = lax.dynamic_index_in_dim(element_counts, chain_at, 1, keepdims=False)
        return (rebalance(sectioned, loads), rebalance(level_here, loads))
    columns, level_columns = lax.map(column, jnp.arange(chain_count, dtype=jnp.int32))
    return (jnp.moveaxis(columns, 0, 1), jnp.moveaxis(level_columns, 0, 1))
```

```python
import functools

import jax
import jax.numpy as jnp
from jax import lax
from jax.experimental import pallas as pl
from jax.experimental.pallas import tpu as pltpu
from jax.sharding import PartitionSpec as P

HOP = 4


HEAT_RATIO = 1.4
TIME_STEP = 0.08
FACE_AXES = (2, 2, 1, 1)
FACE_SIGNS = (-1.0, 1.0, -1.0, 1.0)


def from_partner(block, axis, distance):
    count = lax.axis_size(axis)
    route = []
    for low in range(count):
        high = low | 1 << distance
        if high != low and high < count:
            route += [(low, high), (high, low)]
    return lax.ppermute(block, axis, route)


def send_window(values, staying, capacity):
    slot_count = values.shape[-1]
    start = jnp.minimum(staying, slot_count - capacity)
    return lax.dynamic_slice_in_dim(values, start, capacity, axis=values.ndim - 1)


def land_window(values, received, keep, arriving, partner_staying, capacity):
    slot_axis = values.ndim - 1
    slot_count = values.shape[-1]
    shift = partner_staying - jnp.minimum(partner_staying, slot_count - capacity)
    target = jnp.minimum(keep, slot_count - capacity)
    zero_rows = jnp.zeros(received.shape[:-1] + (capacity,), received.dtype)
    padded = jnp.concatenate([zero_rows, received, zero_rows], axis=slot_axis)
    aligned = lax.dynamic_slice_in_dim(
        padded, capacity + shift - (keep - target), capacity, axis=slot_axis
    )
    position = jnp.arange(slot_count, dtype=jnp.int32)
    kept = jnp.where(position < keep, values, jnp.zeros_like(values))
    region = lax.dynamic_slice_in_dim(kept, target, capacity, axis=slot_axis)
    slot_here = target + jnp.arange(capacity, dtype=jnp.int32)
    update = jnp.where((slot_here >= keep) & (slot_here < keep + arriving), aligned, region)
    return lax.dynamic_update_slice_in_dim(kept, update, target, axis=slot_axis)


def migrate(values, levels, current):
    slot_count = values.shape[-1]
    capacity = slot_count // 4
    rounds_count = lax.axis_size("cube").bit_length() - 1
    for exponent in range(rounds_count):
        partner = from_partner(jnp.reshape(current, (1,)), "cube", exponent)[0]
        leaving = jnp.maximum(current - partner, 0) // 2
        arriving = jnp.maximum(partner - current, 0) // 2
        staying = current - leaving
        partner_staying = partner - arriving
        out_values = send_window(values, staying, capacity)
        out_levels = send_window(levels, staying, capacity)
        in_values, in_levels = from_partner((out_values, out_levels), "cube", exponent)
        values = land_window(values, in_values, staying, arriving, partner_staying, capacity)
        levels = land_window(levels, in_levels, staying, arriving, partner_staying, capacity)
        current = staying + arriving
    return (values, levels, current)


def primitives(w):
    inv = 1.0 / w[0]
    kinetic = w[1] * w[1] + w[2] * w[2] + w[3] * w[3]
    pressure = (HEAT_RATIO - 1.0) * (w[4] - 0.5 * kinetic * inv)
    return inv, pressure


def flux(w, inv, pressure, axis_id):
    momentum = w[1 + axis_id]
    velocity = momentum * inv
    pieces = [momentum]
    for column in range(3):
        component = w[1 + column] * velocity
        if column == axis_id:
            component = component + pressure
        pieces.append(component)
    pieces.append((w[4] + pressure) * velocity)
    return pieces, velocity


def face_jump(inner, neighbour, axis_id, orient):
    inner_inv, inner_press = primitives(inner)
    outer_inv, outer_press = primitives(neighbour)
    inner_flux, inner_vel = flux(inner, inner_inv, inner_press, axis_id)
    outer_flux, outer_vel = flux(neighbour, outer_inv, outer_press, axis_id)
    half_speed = 0.5 * jnp.maximum(
        jnp.abs(inner_vel) + jnp.sqrt(HEAT_RATIO * inner_press * inner_inv),
        jnp.abs(outer_vel) + jnp.sqrt(HEAT_RATIO * outer_press * outer_inv),
    )
    return [
        (0.5 * orient) * (inner_flux[f] - outer_flux[f]) + half_speed * (neighbour[f] - inner[f])
        for f in range(5)
    ]


def signed_jump(inner, neighbour, vertical, orient):
    def side(w):
        inv, pressure = primitives(w)
        momentum = jnp.where(vertical, w[3], w[2])
        velocity = momentum * inv
        along_y = jnp.where(vertical, 0.0, pressure)
        along_z = jnp.where(vertical, pressure, 0.0)
        pieces = [
            momentum,
            w[1] * velocity,
            w[2] * velocity + along_y,
            w[3] * velocity + along_z,
            (w[4] + pressure) * velocity,
        ]
        return pieces, jnp.abs(velocity) + jnp.sqrt(HEAT_RATIO * pressure * inv)

    inner_flux, inner_speed = side(inner)
    outer_flux, outer_speed = side(neighbour)
    half_speed = 0.5 * jnp.maximum(inner_speed, outer_speed)
    half_sign = 0.5 * orient
    return [
        half_sign * (inner_flux[f] - outer_flux[f]) + half_speed * (neighbour[f] - inner[f])
        for f in range(5)
    ]


def section_kernel(
    pairs,
    chain,
    cons_hbm,
    links_hbm,
    levels_hbm,
    counts,
    deriv_hbm,
    lift_hbm,
    done,
    out_levels,
    lift,
    third_pre,
    third_jmp,
    cons,
    links,
    levels,
    deriv,
    own,
    nb,
    hot,
    fluxes,
    pre,
    jmp,
    moved,
    moved_levels,
    leaving,
    arrived,
    load_sems,
    send_sems,
    recv_sems,
    ready_sems,
):
    slots = cons.shape[-1]
    tile = slots // 4
    mesh_id = pl.DeviceIdType.MESH
    c = lax.axis_index("cube")
    h = lax.axis_index("chain")
    last_link = chain - 1
    lowest = h < HOP
    highest = h >= chain - HOP
    ahead = (c, lax.rem(h + 1, chain))
    behind = (c, lax.rem(h + chain - 1, chain))
    hop_ahead = (c, lax.rem(h + HOP, chain))
    hop_behind = (c, lax.rem(h + chain - HOP, chain))
    partner = (1 - c, h)

    def signal(semaphore, device):
        pl.semaphore_signal(semaphore, inc=1, device_id=device, device_id_type=mesh_id)

    barrier = pltpu.get_barrier_semaphore()
    signal(barrier, behind)
    signal(barrier, hop_behind)
    if pairs:
        signal(barrier, partner)

    @pl.when(h < last_link)
    def _():
        signal(barrier, ahead)

    @pl.when(jnp.logical_not(highest))
    def _():
        signal(barrier, hop_ahead)

    fields = []
    for f in range(5):
        load = pltpu.make_async_copy(cons_hbm.at[f], cons.at[f], load_sems.at[4 + f])
        load.start()
        fields.append(load)
    loads = []
    for index, (source, target) in enumerate(
        ((links_hbm, links), (levels_hbm, levels), (deriv_hbm, deriv), (lift_hbm, lift))
    ):
        load = pltpu.make_async_copy(source, target, load_sems.at[index])
        load.start()
        loads.append(load)

    def remote(source, target, index, device):
        return pltpu.make_async_remote_copy(
            src_ref=source,
            dst_ref=target,
            send_sem=send_sems.at[index],
            recv_sem=recv_sems.at[index],
            device_id=device,
            device_id_type=mesh_id,
        )

    row = lax.broadcasted_iota(jnp.int32, (32, 64), 0)
    col = lax.broadcasted_iota(jnp.int32, (32, 64), 1)
    inside = lax.rem(row, 16)
    node = (inside // 4) * 16 + lax.rem(inside, 4) + jnp.where(row >= 16, 12, 0)
    picker = jnp.where(col == node, 1.0, 0.0).astype(jnp.bfloat16)

    for f in range(5):
        fields[f].wait()
        both = jnp.dot(picker, cons[f], preferred_element_type=jnp.float32)
        both = both.astype(jnp.bfloat16)
        own[2, f] = both[0:16]
        own[3, f] = both[16:32]

    copies = [
        remote(cons.at[:, 48:64, :], nb.at[0], 0, ahead),
        remote(cons.at[:, 0:16, :], nb.at[1], 1, behind),
        remote(own.at[3], nb.at[2], 2, hop_ahead),
        remote(own.at[2], nb.at[3], 3, hop_behind),
    ]
    few = jnp.where(h == 0, 1, 0) + jnp.where(lowest, 1, 0)
    pl.semaphore_wait(barrier, (5 if pairs else 4) - few)

    @pl.when(h == last_link)
    def _():
        signal(ready_sems.at[0], ahead)

    @pl.when(highest)
    def _():
        signal(ready_sems.at[1], hop_ahead)
        copies[2].start()

    copies[0].start()

    @pl.when(h > 0)
    def _():
        copies[1].start()

    @pl.when(jnp.logical_not(lowest))
    def _():
        copies[3].start()

    @pl.when(jnp.logical_not(highest))
    def _():
        copies[2].start()

    if pairs:
        moved_copy = remote(cons.at[:, :, 3 * tile :], moved, 4, partner)
        level_copy = remote(levels.at[:, 3 * tile :], moved_levels, 5, partner)
        moved_copy.start()
        loads[1].wait()
        level_copy.start()
    else:
        loads[1].wait()
    loads[0].wait()

    rows_step = 128
    lanes = lax.broadcasted_iota(jnp.int32, (rows_step, tile), 0)

    def columns(t):
        return pl.ds(pl.multiple_of(t * tile, tile), tile)

    def build(face):
        def step(t, carry):
            cols = columns(t)
            link = links[face : face + 1, cols]
            for r in range(0, slots, rows_step):
                hot[face, r : r + rows_step, cols] = jnp.where(
                    lanes == link - r, 1.0, 0.0
                ).astype(jnp.bfloat16)
            return carry

        lax.fori_loop(0, 4, step, 0)

    build(0)
    build(1)

    @pl.when(h == 0)
    def _():
        pl.semaphore_wait(ready_sems.at[0], 1)
        copies[1].start()

    @pl.when(lowest)
    def _():
        pl.semaphore_wait(ready_sems.at[1], 1)
        copies[3].start()

    build(2)
    build(3)
    for f in range(5):
        own[0, f] = cons[f, 0:16, :]
        own[1, f] = cons[f, 48:64, :]
    loads[2].wait()
    loads[3].wait()

    operator = jnp.concatenate([deriv[0], deriv[1], deriv[2]], axis=1)

    def node_fluxes(w, n):
        inv, pressure = primitives(w)
        for d in range(3):
            pieces, _ = flux(w, inv, pressure, d)
            for f in range(5):
                fluxes[f, 64 * d + n : 64 * d + n + 16, :] = pieces[f].astype(jnp.bfloat16)

    def scale_of(block):
        return TIME_STEP * (jnp.int32(1) << block).astype(jnp.float32)

    def volume_step(t, carry):
        cols = columns(t)
        for n in range(0, 64, 16):
            node_fluxes([cons[f, n : n + 16, cols].astype(jnp.float32) for f in range(5)], n)
        factor = scale_of(levels[:, cols])
        for f in range(5):
            volume = jnp.dot(operator, fluxes[f], preferred_element_type=jnp.float32)
            pre[f, :, cols] = cons[f, :, cols].astype(jnp.float32) - factor * volume
        return carry

    def jump_tile(face, cols):
        source = nb[face].reshape(80, slots)
        picked = jnp.dot(source, hot[face, :, cols], preferred_element_type=jnp.float32)
        neighbour = [picked[16 * f : 16 * f + 16] for f in range(5)]
        inner = [own[face, f, :, cols].astype(jnp.float32) for f in range(5)]
        orient = jnp.where(lax.rem(face, 2) == 0, -1.0, 1.0)
        jumps = signed_jump(inner, neighbour, face < 2, orient)
        return [jump.astype(jnp.bfloat16) for jump in jumps]

    def face_rows(face):
        return pl.ds(pl.multiple_of(16 * face, 16), 16)

    def keep_jumps(face, count):
        def step(t, carry):
            cols = columns(t)
            jumps = jump_tile(face, cols)
            for f in range(5):
                jmp[f, face_rows(face), cols] = jumps[f]
            return carry

        lax.fori_loop(0, count, step, 0)

    def finish(cols):
        factor = scale_of(levels[:, cols])
        for f in range(5):
            surface = jnp.dot(lift[...], jmp[f, :, cols], preferred_element_type=jnp.float32)
            done[f, :, cols] = (pre[f, :, cols] + factor * surface).astype(jnp.bfloat16)

    def finish_step(t, carry):
        finish(columns(t))
        return carry

    def wait_face(face):
        remote(own.at[face], nb.at[face], face, partner).wait_recv()

    inner_face = jnp.where(lax.rem(h, 2) == 0, 1, 0)
    if not pairs:
        lax.fori_loop(0, 4, volume_step, 0)

        def whole_face(face, carry):
            wait_face(face)
            keep_jumps(face, 4)
            return carry

        lax.fori_loop(0, 4, whole_face, 0)
        lax.fori_loop(0, 4, finish_step, 0)
        out_levels[...] = levels[...]
        third_pre[...] = jnp.zeros_like(third_pre)
        third_jmp[...] = jnp.zeros_like(third_jmp)
        for copy in copies:
            copy.wait_send()
        return

    last = pl.ds(3 * tile, tile)
    third = pl.ds(2 * tile, tile)

    def choose(mine, other):
        full = jnp.broadcast_to(counts[0, 0], mine.shape) == slots
        chosen = jnp.where(full, mine.astype(jnp.float32), other.astype(jnp.float32))
        return chosen.astype(mine.dtype)

    def jump_copy(face):
        return remote(leaving.at[face], arrived.at[face], 6 + face, partner)

    def begin(face):
        wait_face(face)
        jumps = jump_tile(face, last)
        for f in range(5):
            leaving[face, f] = jumps[f]
        jump_copy(face).start()
        keep_jumps(face, 3)

    def settle(face):
        jump_copy(face).wait_recv()
        for f in range(5):
            mine = jmp[f, face_rows(face), third]
            third_jmp[f, face_rows(face), :] = choose(mine, arrived[face, f])

    order = [inner_face, 1 - inner_face, jnp.int32(2), jnp.int32(3)]
    order[1] = jnp.where(h == 0, 2, order[1])
    order[2] = jnp.where(h == 0, 0, order[2])

    lax.fori_loop(0, 2, volume_step, 0)
    begin(order[0])
    out_levels[:, 0 : 2 * tile] = levels[:, 0 : 2 * tile]
    out_levels[:, last] = jnp.zeros((1, tile), jnp.int32)

    level_copy.wait_recv()
    full_row = jnp.broadcast_to(counts[0, 0], (1, tile)) == slots
    chosen_levels = jnp.where(full_row, levels[:, third], moved_levels[...])
    out_levels[:, third] = chosen_levels
    factor = scale_of(chosen_levels)
    moved_copy.wait_recv()
    for n in range(0, 64, 16):
        w = []
        for f in range(5):
            chosen = choose(cons[f, n : n + 16, third], moved[f, n : n + 16, :])
            w.append(chosen.astype(jnp.float32))
            third_pre[f, n : n + 16, :] = w[f]
        node_fluxes(w, n)
    for f in range(5):
        volume = jnp.dot(operator, fluxes[f], preferred_element_type=jnp.float32)
        third_pre[f] = third_pre[f] - factor * volume

    settle(order[0])
    begin(order[1])
    begin(order[2])
    settle(order[1])
    begin(order[3])
    settle(order[2])
    lax.fori_loop(0, 2, finish_step, 0)
    settle(order[3])
    for copy in copies + [moved_copy, level_copy] + [jump_copy(face) for face in range(4)]:
        copy.wait_send()


def write_kernel(done, levels, lift, pre, jmp, out, out_levels, fresh, blank, sems):
    tile = pre.shape[-1]
    copies = [
        pltpu.make_async_copy(done, out.at[:, :, 0 : 2 * tile], sems.at[0]),
        pltpu.make_async_copy(levels, out_levels, sems.at[1]),
        pltpu.make_async_copy(blank, out.at[:, :, 3 * tile :], sems.at[2]),
    ]
    copies[0].start()
    copies[1].start()
    factor = TIME_STEP * (jnp.int32(1) << levels[:, 2 * tile : 3 * tile]).astype(jnp.float32)
    for f in range(5):
        surface = jnp.dot(lift[...], jmp[f], preferred_element_type=jnp.float32)
        fresh[f] = (pre[f] + factor * surface).astype(jnp.bfloat16)
        copy = pltpu.make_async_copy(
            fresh.at[f], out.at[f, :, 2 * tile : 3 * tile], sems.at[3 + f]
        )
        copy.start()
        copies.append(copy)
    blank[...] = jnp.zeros_like(blank)
    copies[2].start()
    for copy in copies:
        copy.wait()


def stay(block):
    return pltpu.with_memory_space_constraint(block, pltpu.HBM)


def per_device(conserved, element_counts, face_links, refinement, derivative, face_lift):
    slots = conserved.shape[-1]
    tile = slots // 4
    pairs = lax.axis_size("cube") == 2
    vmem = pl.BlockSpec(memory_space=pltpu.VMEM)
    hbm = pl.BlockSpec(memory_space=pltpu.HBM)
    smem = pl.BlockSpec(memory_space=pltpu.SMEM)
    half = jnp.bfloat16
    kept = 2 * tile if pairs else slots
    parts = pl.pallas_call(
        functools.partial(section_kernel, pairs, lax.axis_size("chain")),
        out_shape=(
            jax.ShapeDtypeStruct((5, 64, kept), half),
            jax.ShapeDtypeStruct((1, slots), jnp.int32),
            jax.ShapeDtypeStruct((64, 64), half),
            jax.ShapeDtypeStruct((5, 64, tile), jnp.float32),
            jax.ShapeDtypeStruct((5, 64, tile), half),
        ),
        in_specs=[hbm, hbm, hbm, smem, hbm, hbm],
        out_specs=(vmem,) * 5,
        scratch_shapes=[
            pltpu.VMEM((5, 64, slots), half),
            pltpu.VMEM((4, slots), jnp.int32),
            pltpu.VMEM((1, slots), jnp.int32),
            pltpu.VMEM((3, 64, 64), half),
            pltpu.VMEM((4, 5, 16, slots), half),
            pltpu.VMEM((4, 5, 16, slots), half),
            pltpu.VMEM((4, slots, slots), half),
            pltpu.VMEM((5, 192, tile), half),
            pltpu.VMEM((5, 64, slots), jnp.float32),
            pltpu.VMEM((5, 64, slots), half),
            pltpu.VMEM((5, 64, tile), half),
            pltpu.VMEM((1, tile), jnp.int32),
            pltpu.VMEM((4, 5, 16, tile), half),
            pltpu.VMEM((4, 5, 16, tile), half),
            pltpu.SemaphoreType.DMA((9,)),
            pltpu.SemaphoreType.DMA((10,)),
            pltpu.SemaphoreType.DMA((10,)),
            pltpu.SemaphoreType.REGULAR((2,)),
        ],
        compiler_params=pltpu.CompilerParams(
            collective_id=0, has_side_effects=True, vmem_limit_bytes=40 << 20
        ),
    )(
        stay(conserved[0, 0]),
        stay(face_links[0, 0]),
        stay(refinement[0]),
        element_counts,
        stay(derivative),
        stay(face_lift),
    )
    if pairs:
        fresh, levels = pl.pallas_call(
            write_kernel,
            out_shape=(
                jax.ShapeDtypeStruct((5, 64, slots), half),
                jax.ShapeDtypeStruct((1, slots), jnp.int32),
            ),
            in_specs=[vmem] * 5,
            out_specs=(hbm, hbm),
            scratch_shapes=[
                pltpu.VMEM((5, 64, tile), half),
                pltpu.VMEM((5, 64, tile), half),
                pltpu.SemaphoreType.DMA((8,)),
            ],
            compiler_params=pltpu.CompilerParams(vmem_limit_bytes=8 << 20),
        )(*parts)
    else:
        fresh, moved, _ = migrate(
            parts[0], parts[1][0].astype(jnp.bfloat16), element_counts[0, 0]
        )
        levels = moved.astype(jnp.int32)[None]
    return (fresh[None, None], levels[None])


def solution(mesh):
    placed = (
        P("cube", "chain", None, None, None),
        P("cube", "chain"),
        P("cube", "chain", None, None),
        P("cube", "chain", None),
        P(),
        P(),
    )
    return jax.shard_map(
        per_device,
        mesh=mesh,
        in_specs=placed,
        out_specs=(P("cube", "chain", None, None, None), P("cube", "chain", None)),
        check_vma=False,
    )
```

```python
import functools

import jax
import jax.numpy as jnp
from jax import lax
from jax.experimental import pallas as pl
from jax.experimental.pallas import tpu as pltpu
from jax.sharding import PartitionSpec as P

HOP = 4


HEAT_RATIO = 1.4
TIME_STEP = 0.08
FACE_AXES = (2, 2, 1, 1)
FACE_SIGNS = (-1.0, 1.0, -1.0, 1.0)


def from_partner(block, axis, distance):
    count = lax.axis_size(axis)
    route = []
    for low in range(count):
        high = low | 1 << distance
        if high != low and high < count:
            route += [(low, high), (high, low)]
    return lax.ppermute(block, axis, route)


def send_window(values, staying, capacity):
    slot_count = values.shape[-1]
    start = jnp.minimum(staying, slot_count - capacity)
    return lax.dynamic_slice_in_dim(values, start, capacity, axis=values.ndim - 1)


def land_window(values, received, keep, arriving, partner_staying, capacity):
    slot_axis = values.ndim - 1
    slot_count = values.shape[-1]
    shift = partner_staying - jnp.minimum(partner_staying, slot_count - capacity)
    target = jnp.minimum(keep, slot_count - capacity)
    zero_rows = jnp.zeros(received.shape[:-1] + (capacity,), received.dtype)
    padded = jnp.concatenate([zero_rows, received, zero_rows], axis=slot_axis)
    aligned = lax.dynamic_slice_in_dim(
        padded, capacity + shift - (keep - target), capacity, axis=slot_axis
    )
    position = jnp.arange(slot_count, dtype=jnp.int32)
    kept = jnp.where(position < keep, values, jnp.zeros_like(values))
    region = lax.dynamic_slice_in_dim(kept, target, capacity, axis=slot_axis)
    slot_here = target + jnp.arange(capacity, dtype=jnp.int32)
    update = jnp.where((slot_here >= keep) & (slot_here < keep + arriving), aligned, region)
    return lax.dynamic_update_slice_in_dim(kept, update, target, axis=slot_axis)


def migrate(values, levels, current):
    slot_count = values.shape[-1]
    capacity = slot_count // 4
    rounds_count = lax.axis_size("cube").bit_length() - 1
    for exponent in range(rounds_count):
        partner = from_partner(jnp.reshape(current, (1,)), "cube", exponent)[0]
        leaving = jnp.maximum(current - partner, 0) // 2
        arriving = jnp.maximum(partner - current, 0) // 2
        staying = current - leaving
        partner_staying = partner - arriving
        out_values = send_window(values, staying, capacity)
        out_levels = send_window(levels, staying, capacity)
        in_values, in_levels = from_partner((out_values, out_levels), "cube", exponent)
        values = land_window(values, in_values, staying, arriving, partner_staying, capacity)
        levels = land_window(levels, in_levels, staying, arriving, partner_staying, capacity)
        current = staying + arriving
    return (values, levels, current)


def primitives(w):
    inv = 1.0 / w[0]
    kinetic = w[1] * w[1] + w[2] * w[2] + w[3] * w[3]
    pressure = (HEAT_RATIO - 1.0) * (w[4] - 0.5 * kinetic * inv)
    return inv, pressure


def flux(w, inv, pressure, axis_id):
    momentum = w[1 + axis_id]
    velocity = momentum * inv
    pieces = [momentum]
    for column in range(3):
        component = w[1 + column] * velocity
        if column == axis_id:
            component = component + pressure
        pieces.append(component)
    pieces.append((w[4] + pressure) * velocity)
    return pieces, velocity


def face_jump(inner, neighbour, axis_id, orient):
    inner_inv, inner_press = primitives(inner)
    outer_inv, outer_press = primitives(neighbour)
    inner_flux, inner_vel = flux(inner, inner_inv, inner_press, axis_id)
    outer_flux, outer_vel = flux(neighbour, outer_inv, outer_press, axis_id)
    half_speed = 0.5 * jnp.maximum(
        jnp.abs(inner_vel) + jnp.sqrt(HEAT_RATIO * inner_press * inner_inv),
        jnp.abs(outer_vel) + jnp.sqrt(HEAT_RATIO * outer_press * outer_inv),
    )
    return [
        (0.5 * orient) * (inner_flux[f] - outer_flux[f]) + half_speed * (neighbour[f] - inner[f])
        for f in range(5)
    ]


def signed_jump(inner, neighbour, vertical, orient):
    def side(w):
        inv, pressure = primitives(w)
        momentum = jnp.where(vertical, w[3], w[2])
        velocity = momentum * inv
        along_y = jnp.where(vertical, 0.0, pressure)
        along_z = jnp.where(vertical, pressure, 0.0)
        pieces = [
            momentum,
            w[1] * velocity,
            w[2] * velocity + along_y,
            w[3] * velocity + along_z,
            (w[4] + pressure) * velocity,
        ]
        return pieces, jnp.abs(velocity) + jnp.sqrt(HEAT_RATIO * pressure * inv)

    inner_flux, inner_speed = side(inner)
    outer_flux, outer_speed = side(neighbour)
    half_speed = 0.5 * jnp.maximum(inner_speed, outer_speed)
    half_sign = 0.5 * orient
    return [
        half_sign * (inner_flux[f] - outer_flux[f]) + half_speed * (neighbour[f] - inner[f])
        for f in range(5)
    ]


def section_kernel(
    pairs,
    chain,
    cons_hbm,
    links_hbm,
    levels_hbm,
    counts,
    deriv_hbm,
    lift_hbm,
    done,
    out_levels,
    lift,
    third_pre,
    third_jmp,
    cons,
    links,
    levels,
    deriv,
    own,
    nb,
    hot,
    fluxes,
    pre,
    jmp,
    moved,
    moved_levels,
    leaving,
    arrived,
    asking,
    asked,
    serving,
    served,
    crossed,
    third_own,
    load_sems,
    send_sems,
    recv_sems,
    ready_sems,
):
    slots = cons.shape[-1]
    tile = slots // 4
    mesh_id = pl.DeviceIdType.MESH
    c = lax.axis_index("cube")
    h = lax.axis_index("chain")
    last_link = chain - 1
    lowest = h < HOP
    highest = h >= chain - HOP
    ahead = (c, lax.rem(h + 1, chain))
    behind = (c, lax.rem(h + chain - 1, chain))
    hop_ahead = (c, lax.rem(h + HOP, chain))
    hop_behind = (c, lax.rem(h + chain - HOP, chain))
    partner = (1 - c, h)
    cross_ahead = (1 - c, lax.rem(h + HOP, chain))
    cross_behind = (1 - c, lax.rem(h + chain - HOP, chain))

    def signal(semaphore, device):
        pl.semaphore_signal(semaphore, inc=1, device_id=device, device_id_type=mesh_id)

    barrier = pltpu.get_barrier_semaphore()
    signal(barrier, behind)
    signal(barrier, hop_behind)
    if pairs:
        signal(barrier, partner)

        @pl.when(lowest)
        def _():
            signal(barrier, cross_behind)

    @pl.when(h < last_link)
    def _():
        signal(barrier, ahead)

    @pl.when(jnp.logical_not(highest))
    def _():
        signal(barrier, hop_ahead)
        if pairs:
            signal(barrier, cross_ahead)

    fields = []
    for f in range(5):
        load = pltpu.make_async_copy(cons_hbm.at[f], cons.at[f], load_sems.at[4 + f])
        load.start()
        fields.append(load)
    loads = []
    for index, (source, target) in enumerate(
        ((links_hbm, links), (levels_hbm, levels), (deriv_hbm, deriv), (lift_hbm, lift))
    ):
        load = pltpu.make_async_copy(source, target, load_sems.at[index])
        load.start()
        loads.append(load)

    def remote(source, target, index, device):
        return pltpu.make_async_remote_copy(
            src_ref=source,
            dst_ref=target,
            send_sem=send_sems.at[index],
            recv_sem=recv_sems.at[index],
            device_id=device,
            device_id_type=mesh_id,
        )

    row = lax.broadcasted_iota(jnp.int32, (32, 64), 0)
    col = lax.broadcasted_iota(jnp.int32, (32, 64), 1)
    inside = lax.rem(row, 16)
    node = (inside // 4) * 16 + lax.rem(inside, 4) + jnp.where(row >= 16, 12, 0)
    picker = jnp.where(col == node, 1.0, 0.0).astype(jnp.bfloat16)

    for f in range(5):
        fields[f].wait()
        both = jnp.dot(picker, cons[f], preferred_element_type=jnp.float32)
        both = both.astype(jnp.bfloat16)
        own[2, f] = both[0:16]
        own[3, f] = both[16:32]

    copies = [
        remote(cons.at[:, 48:64, :], nb.at[0], 0, ahead),
        remote(cons.at[:, 0:16, :], nb.at[1], 1, behind),
        remote(own.at[3], nb.at[2], 2, hop_ahead),
    ]
    if pairs:
        ask = remote(asking, asked, 3, hop_ahead)
        serve = remote(serving.at[:, :, 0 : 3 * tile], served, 9, hop_behind)
        serve_cross = remote(serving.at[:, :, 3 * tile :], crossed, 10, cross_behind)
    else:
        copies.append(remote(own.at[2], nb.at[3], 3, hop_behind))
    loads[0].wait()
    asking[...] = links[3:4, :]
    expected = 6 if pairs else 4
    expected -= jnp.where(h == 0, 1, 0) + jnp.where(lowest, 2 if pairs else 1, 0)
    if pairs:
        expected += jnp.where(highest, 1, 0)
    pl.semaphore_wait(barrier, expected)

    if pairs:
        ask.start()

    @pl.when(h == last_link)
    def _():
        signal(ready_sems.at[0], ahead)
        copies[0].start()

    @pl.when(highest)
    def _():
        signal(ready_sems.at[1], hop_ahead)
        if pairs:
            signal(ready_sems.at[1], cross_ahead)
        copies[2].start()

    @pl.when(h < last_link)
    def _():
        copies[0].start()

    @pl.when(h > 0)
    def _():
        copies[1].start()

    @pl.when(jnp.logical_not(highest))
    def _():
        copies[2].start()

    if pairs:
        moved_copy = remote(cons.at[:, :, 3 * tile :], moved, 4, partner)
        level_copy = remote(levels.at[:, 3 * tile :], moved_levels, 5, partner)
        moved_copy.start()
        loads[1].wait()
        level_copy.start()
    else:
        loads[1].wait()

        @pl.when(jnp.logical_not(lowest))
        def _():
            copies[3].start()

    rows_step = 128
    lanes = lax.broadcasted_iota(jnp.int32, (rows_step, tile), 0)

    def columns(t):
        return pl.ds(pl.multiple_of(t * tile, tile), tile)

    def build_tile(face, link, cols):
        for r in range(0, slots, rows_step):
            hot[face, r : r + rows_step, cols] = jnp.where(
                lanes == link - r, 1.0, 0.0
            ).astype(jnp.bfloat16)

    def build(face):
        def step(t, carry):
            cols = columns(t)
            build_tile(face, links[face : face + 1, cols], cols)
            return carry

        lax.fori_loop(0, 4, step, 0)

    build(0)
    build(1)

    @pl.when(h == 0)
    def _():
        pl.semaphore_wait(ready_sems.at[0], 1)
        copies[1].start()

    if not pairs:

        @pl.when(lowest)
        def _():
            pl.semaphore_wait(ready_sems.at[1], 1)
            copies[3].start()

    build(2)
    if not pairs:
        build(3)
    for f in range(5):
        own[0, f] = cons[f, 0:16, :]
        own[1, f] = cons[f, 48:64, :]
    loads[2].wait()
    loads[3].wait()

    operator = jnp.concatenate([deriv[0], deriv[1], deriv[2]], axis=1)

    def node_fluxes(w, n):
        inv, pressure = primitives(w)
        for d in range(3):
            pieces, _ = flux(w, inv, pressure, d)
            for f in range(5):
                fluxes[f, 64 * d + n : 64 * d + n + 16, :] = pieces[f].astype(jnp.bfloat16)

    def scale_of(block):
        return TIME_STEP * (jnp.int32(1) << block).astype(jnp.float32)

    def volume_step(t, carry):
        cols = columns(t)
        for n in range(0, 64, 16):
            node_fluxes([cons[f, n : n + 16, cols].astype(jnp.float32) for f in range(5)], n)
        factor = scale_of(levels[:, cols])
        for f in range(5):
            volume = jnp.dot(operator, fluxes[f], preferred_element_type=jnp.float32)
            pre[f, :, cols] = cons[f, :, cols].astype(jnp.float32) - factor * volume
        return carry

    def jump_tile(face, cols):
        source = nb[face].reshape(80, slots)
        picked = jnp.dot(source, hot[face, :, cols], preferred_element_type=jnp.float32)
        neighbour = [picked[16 * f : 16 * f + 16] for f in range(5)]
        inner = [own[face, f, :, cols].astype(jnp.float32) for f in range(5)]
        orient = jnp.where(lax.rem(face, 2) == 0, -1.0, 1.0)
        jumps = signed_jump(inner, neighbour, face < 2, orient)
        return [jump.astype(jnp.bfloat16) for jump in jumps]

    def face_rows(face):
        return pl.ds(pl.multiple_of(16 * face, 16), 16)

    def keep_jumps(face, count):
        def step(t, carry):
            cols = columns(t)
            jumps = jump_tile(face, cols)
            for f in range(5):
                jmp[f, face_rows(face), cols] = jumps[f]
            return carry

        lax.fori_loop(0, count, step, 0)

    def finish(cols):
        factor = scale_of(levels[:, cols])
        for f in range(5):
            surface = jnp.dot(lift[...], jmp[f, :, cols], preferred_element_type=jnp.float32)
            done[f, :, cols] = (pre[f, :, cols] + factor * surface).astype(jnp.bfloat16)

    def finish_step(t, carry):
        finish(columns(t))
        return carry

    def wait_face(face):
        remote(own.at[face], nb.at[face], face, partner).wait_recv()

    inner_face = jnp.where(lax.rem(h, 2) == 0, 1, 0)
    if not pairs:
        lax.fori_loop(0, 4, volume_step, 0)

        def whole_face(face, carry):
            wait_face(face)
            keep_jumps(face, 4)
            return carry

        lax.fori_loop(0, 4, whole_face, 0)
        lax.fori_loop(0, 4, finish_step, 0)
        out_levels[...] = levels[...]
        third_pre[...] = jnp.zeros_like(third_pre)
        third_jmp[...] = jnp.zeros_like(third_jmp)
        for copy in copies:
            copy.wait_send()
        return

    last = pl.ds(3 * tile, tile)
    third = pl.ds(2 * tile, tile)

    def choose(mine, other):
        full = jnp.broadcast_to(counts[0, 0], mine.shape) == slots
        chosen = jnp.where(full, mine.astype(jnp.float32), other.astype(jnp.float32))
        return chosen.astype(mine.dtype)

    def serve_tile(t, carry):
        cols = columns(t)
        build_tile(3, asked[:, cols], cols)
        source = own[2].reshape(80, slots)
        picked = jnp.dot(source, hot[3, :, cols], preferred_element_type=jnp.float32)
        for f in range(5):
            serving[f, :, cols] = picked[16 * f : 16 * f + 16].astype(jnp.bfloat16)
        return carry

    def answer():
        ask.wait_recv()
        serve_tile(jnp.int32(3), 0)

        @pl.when(lowest)
        def _():
            pl.semaphore_wait(ready_sems.at[1], 2)

        serve_cross.start()
        lax.fori_loop(0, 3, serve_tile, 0)
        serve.start()

    def jump_copy(face):
        return remote(leaving.at[face], arrived.at[face], 6 + face, partner)

    def begin(face):
        wait_face(face)
        jumps = jump_tile(face, last)
        for f in range(5):
            leaving[face, f] = jumps[f]
        jump_copy(face).start()
        keep_jumps(face, 3)

    def settle(face):
        jump_copy(face).wait_recv()
        for f in range(5):
            mine = jmp[f, face_rows(face), third]
            third_jmp[f, face_rows(face), :] = choose(mine, arrived[face, f])

    def served_jumps(inner, neighbour):
        inner = [u.astype(jnp.float32) for u in inner]
        neighbour = [w.astype(jnp.float32) for w in neighbour]
        jumps = face_jump(inner, neighbour, FACE_AXES[3], FACE_SIGNS[3])
        return [jump.astype(jnp.bfloat16) for jump in jumps]

    def served_step(t, carry):
        cols = columns(t)
        jumps = served_jumps(
            [own[3, f, :, cols] for f in range(5)], [served[f, :, cols] for f in range(5)]
        )
        for f in range(5):
            jmp[f, 48:64, cols] = jumps[f]
        return carry

    order = [inner_face, 1 - inner_face, jnp.int32(2)]
    order[1] = jnp.where(h == 0, 2, order[1])
    order[2] = jnp.where(h == 0, 0, order[2])

    lax.fori_loop(0, 2, volume_step, 0)

    @pl.when(jnp.logical_not(lowest))
    def _():
        answer()

    begin(order[0])

    @pl.when(lowest)
    def _():
        answer()

    out_levels[:, 0 : 2 * tile] = levels[:, 0 : 2 * tile]
    out_levels[:, last] = jnp.zeros((1, tile), jnp.int32)

    level_copy.wait_recv()
    full_row = jnp.broadcast_to(counts[0, 0], (1, tile)) == slots
    chosen_levels = jnp.where(full_row, levels[:, third], moved_levels[...])
    out_levels[:, third] = chosen_levels
    factor = scale_of(chosen_levels)
    moved_copy.wait_recv()
    for n in range(0, 64, 16):
        w = []
        for f in range(5):
            chosen = choose(cons[f, n : n + 16, third], moved[f, n : n + 16, :])
            w.append(chosen.astype(jnp.float32))
            third_pre[f, n : n + 16, :] = w[f]
        node_fluxes(w, n)
    for f in range(5):
        volume = jnp.dot(operator, fluxes[f], preferred_element_type=jnp.float32)
        third_pre[f] = third_pre[f] - factor * volume
        both = jnp.dot(picker, moved[f], preferred_element_type=jnp.float32)
        third_own[f] = choose(own[3, f, :, third], both[16:32].astype(jnp.bfloat16))

    settle(order[0])
    begin(order[1])
    begin(order[2])
    settle(order[1])
    serve.wait_recv()
    lax.fori_loop(0, 2, served_step, 0)
    lax.fori_loop(0, 2, finish_step, 0)
    serve_cross.wait_recv()
    beyond = [choose(served[f, :, third], crossed[f]) for f in range(5)]
    jumps = served_jumps([third_own[f] for f in range(5)], beyond)
    for f in range(5):
        third_jmp[f, 48:64, :] = jumps[f]
    settle(order[2])
    sent = copies + [ask, serve, serve_cross, moved_copy, level_copy]
    for copy in sent + [jump_copy(face) for face in range(3)]:
        copy.wait_send()


def write_kernel(done, levels, lift, pre, jmp, out, out_levels, fresh, blank, sems):
    tile = pre.shape[-1]
    copies = [
        pltpu.make_async_copy(done, out.at[:, :, 0 : 2 * tile], sems.at[0]),
        pltpu.make_async_copy(levels, out_levels, sems.at[1]),
        pltpu.make_async_copy(blank, out.at[:, :, 3 * tile :], sems.at[2]),
    ]
    copies[0].start()
    copies[1].start()
    factor = TIME_STEP * (jnp.int32(1) << levels[:, 2 * tile : 3 * tile]).astype(jnp.float32)
    for f in range(5):
        surface = jnp.dot(lift[...], jmp[f], preferred_element_type=jnp.float32)
        fresh[f] = (pre[f] + factor * surface).astype(jnp.bfloat16)
        copy = pltpu.make_async_copy(
            fresh.at[f], out.at[f, :, 2 * tile : 3 * tile], sems.at[3 + f]
        )
        copy.start()
        copies.append(copy)
    blank[...] = jnp.zeros_like(blank)
    copies[2].start()
    for copy in copies:
        copy.wait()


def stay(block):
    return pltpu.with_memory_space_constraint(block, pltpu.HBM)


def per_device(conserved, element_counts, face_links, refinement, derivative, face_lift):
    slots = conserved.shape[-1]
    tile = slots // 4
    pairs = lax.axis_size("cube") == 2
    vmem = pl.BlockSpec(memory_space=pltpu.VMEM)
    hbm = pl.BlockSpec(memory_space=pltpu.HBM)
    smem = pl.BlockSpec(memory_space=pltpu.SMEM)
    half = jnp.bfloat16
    kept = 2 * tile if pairs else slots
    parts = pl.pallas_call(
        functools.partial(section_kernel, pairs, lax.axis_size("chain")),
        out_shape=(
            jax.ShapeDtypeStruct((5, 64, kept), half),
            jax.ShapeDtypeStruct((1, slots), jnp.int32),
            jax.ShapeDtypeStruct((64, 64), half),
            jax.ShapeDtypeStruct((5, 64, tile), jnp.float32),
            jax.ShapeDtypeStruct((5, 64, tile), half),
        ),
        in_specs=[hbm, hbm, hbm, smem, hbm, hbm],
        out_specs=(vmem,) * 5,
        scratch_shapes=[
            pltpu.VMEM((5, 64, slots), half),
            pltpu.VMEM((4, slots), jnp.int32),
            pltpu.VMEM((1, slots), jnp.int32),
            pltpu.VMEM((3, 64, 64), half),
            pltpu.VMEM((4, 5, 16, slots), half),
            pltpu.VMEM((4, 5, 16, slots), half),
            pltpu.VMEM((4, slots, slots), half),
            pltpu.VMEM((5, 192, tile), half),
            pltpu.VMEM((5, 64, slots), jnp.float32),
            pltpu.VMEM((5, 64, slots), half),
            pltpu.VMEM((5, 64, tile), half),
            pltpu.VMEM((1, tile), jnp.int32),
            pltpu.VMEM((3, 5, 16, tile), half),
            pltpu.VMEM((3, 5, 16, tile), half),
            pltpu.VMEM((1, slots), jnp.int32),
            pltpu.VMEM((1, slots), jnp.int32),
            pltpu.VMEM((5, 16, slots), half),
            pltpu.VMEM((5, 16, 3 * tile), half),
            pltpu.VMEM((5, 16, tile), half),
            pltpu.VMEM((5, 16, tile), half),
            pltpu.SemaphoreType.DMA((9,)),
            pltpu.SemaphoreType.DMA((11,)),
            pltpu.SemaphoreType.DMA((11,)),
            pltpu.SemaphoreType.REGULAR((2,)),
        ],
        compiler_params=pltpu.CompilerParams(
            collective_id=0, has_side_effects=True, vmem_limit_bytes=40 << 20
        ),
    )(
        stay(conserved[0, 0]),
        stay(face_links[0, 0]),
        stay(refinement[0]),
        element_counts,
        stay(derivative),
        stay(face_lift),
    )
    if pairs:
        fresh, levels = pl.pallas_call(
            write_kernel,
            out_shape=(
                jax.ShapeDtypeStruct((5, 64, slots), half),
                jax.ShapeDtypeStruct((1, slots), jnp.int32),
            ),
            in_specs=[vmem] * 5,
            out_specs=(hbm, hbm),
            scratch_shapes=[
                pltpu.VMEM((5, 64, tile), half),
                pltpu.VMEM((5, 64, tile), half),
                pltpu.SemaphoreType.DMA((8,)),
            ],
            compiler_params=pltpu.CompilerParams(vmem_limit_bytes=8 << 20),
        )(*parts)
    else:
        fresh, moved, _ = migrate(
            parts[0], parts[1][0].astype(jnp.bfloat16), element_counts[0, 0]
        )
        levels = moved.astype(jnp.int32)[None]
    return (fresh[None, None], levels[None])


def solution(mesh):
    placed = (
        P("cube", "chain", None, None, None),
        P("cube", "chain"),
        P("cube", "chain", None, None),
        P("cube", "chain", None),
        P(),
        P(),
    )
    return jax.shard_map(
        per_device,
        mesh=mesh,
        in_specs=placed,
        out_specs=(P("cube", "chain", None, None, None), P("cube", "chain", None)),
        check_vma=False,
    )
```

```python
import functools

import jax
import jax.numpy as jnp
from jax import lax
from jax.experimental import pallas as pl
from jax.experimental.pallas import tpu as pltpu
from jax.sharding import PartitionSpec as P

HOP = 4


HEAT_RATIO = 1.4
TIME_STEP = 0.08
FACE_AXES = (2, 2, 1, 1)
FACE_SIGNS = (-1.0, 1.0, -1.0, 1.0)


def from_partner(block, axis, distance):
    count = lax.axis_size(axis)
    route = []
    for low in range(count):
        high = low | 1 << distance
        if high != low and high < count:
            route += [(low, high), (high, low)]
    return lax.ppermute(block, axis, route)


def send_window(values, staying, capacity):
    slot_count = values.shape[-1]
    start = jnp.minimum(staying, slot_count - capacity)
    return lax.dynamic_slice_in_dim(values, start, capacity, axis=values.ndim - 1)


def land_window(values, received, keep, arriving, partner_staying, capacity):
    slot_axis = values.ndim - 1
    slot_count = values.shape[-1]
    shift = partner_staying - jnp.minimum(partner_staying, slot_count - capacity)
    target = jnp.minimum(keep, slot_count - capacity)
    zero_rows = jnp.zeros(received.shape[:-1] + (capacity,), received.dtype)
    padded = jnp.concatenate([zero_rows, received, zero_rows], axis=slot_axis)
    aligned = lax.dynamic_slice_in_dim(
        padded, capacity + shift - (keep - target), capacity, axis=slot_axis
    )
    position = jnp.arange(slot_count, dtype=jnp.int32)
    kept = jnp.where(position < keep, values, jnp.zeros_like(values))
    region = lax.dynamic_slice_in_dim(kept, target, capacity, axis=slot_axis)
    slot_here = target + jnp.arange(capacity, dtype=jnp.int32)
    update = jnp.where((slot_here >= keep) & (slot_here < keep + arriving), aligned, region)
    return lax.dynamic_update_slice_in_dim(kept, update, target, axis=slot_axis)


def migrate(values, levels, current):
    slot_count = values.shape[-1]
    capacity = slot_count // 4
    rounds_count = lax.axis_size("cube").bit_length() - 1
    for exponent in range(rounds_count):
        partner = from_partner(jnp.reshape(current, (1,)), "cube", exponent)[0]
        leaving = jnp.maximum(current - partner, 0) // 2
        arriving = jnp.maximum(partner - current, 0) // 2
        staying = current - leaving
        partner_staying = partner - arriving
        out_values = send_window(values, staying, capacity)
        out_levels = send_window(levels, staying, capacity)
        in_values, in_levels = from_partner((out_values, out_levels), "cube", exponent)
        values = land_window(values, in_values, staying, arriving, partner_staying, capacity)
        levels = land_window(levels, in_levels, staying, arriving, partner_staying, capacity)
        current = staying + arriving
    return (values, levels, current)


def primitives(w):
    inv = 1.0 / w[0]
    kinetic = w[1] * w[1] + w[2] * w[2] + w[3] * w[3]
    pressure = (HEAT_RATIO - 1.0) * (w[4] - 0.5 * kinetic * inv)
    return inv, pressure


def flux(w, inv, pressure, axis_id):
    momentum = w[1 + axis_id]
    velocity = momentum * inv
    pieces = [momentum]
    for column in range(3):
        component = w[1 + column] * velocity
        if column == axis_id:
            component = component + pressure
        pieces.append(component)
    pieces.append((w[4] + pressure) * velocity)
    return pieces, velocity


def face_jump(inner, neighbour, axis_id, orient):
    inner_inv, inner_press = primitives(inner)
    outer_inv, outer_press = primitives(neighbour)
    inner_flux, inner_vel = flux(inner, inner_inv, inner_press, axis_id)
    outer_flux, outer_vel = flux(neighbour, outer_inv, outer_press, axis_id)
    half_speed = 0.5 * jnp.maximum(
        jnp.abs(inner_vel) + jnp.sqrt(HEAT_RATIO * inner_press * inner_inv),
        jnp.abs(outer_vel) + jnp.sqrt(HEAT_RATIO * outer_press * outer_inv),
    )
    return [
        (0.5 * orient) * (inner_flux[f] - outer_flux[f]) + half_speed * (neighbour[f] - inner[f])
        for f in range(5)
    ]


def signed_jump(inner, neighbour, vertical, orient):
    def side(w):
        inv, pressure = primitives(w)
        momentum = jnp.where(vertical, w[3], w[2])
        velocity = momentum * inv
        along_y = jnp.where(vertical, 0.0, pressure)
        along_z = jnp.where(vertical, pressure, 0.0)
        pieces = [
            momentum,
            w[1] * velocity,
            w[2] * velocity + along_y,
            w[3] * velocity + along_z,
            (w[4] + pressure) * velocity,
        ]
        return pieces, jnp.abs(velocity) + jnp.sqrt(HEAT_RATIO * pressure * inv)

    inner_flux, inner_speed = side(inner)
    outer_flux, outer_speed = side(neighbour)
    half_speed = 0.5 * jnp.maximum(inner_speed, outer_speed)
    half_sign = 0.5 * orient
    return [
        half_sign * (inner_flux[f] - outer_flux[f]) + half_speed * (neighbour[f] - inner[f])
        for f in range(5)
    ]


def section_kernel(
    pairs,
    chain,
    cons_hbm,
    links_hbm,
    levels_hbm,
    counts,
    deriv_hbm,
    lift_hbm,
    done,
    out_levels,
    lift,
    third_pre,
    third_jmp,
    cons,
    links,
    levels,
    deriv,
    own,
    nb,
    hot,
    fluxes,
    pre,
    jmp,
    moved,
    moved_levels,
    leaving,
    arrived,
    asking,
    asked,
    serving,
    served,
    crossed,
    third_own,
    load_sems,
    send_sems,
    recv_sems,
    ready_sems,
):
    slots = cons.shape[-1]
    tile = slots // 4
    mesh_id = pl.DeviceIdType.MESH
    c = lax.axis_index("cube")
    h = lax.axis_index("chain")
    last_link = chain - 1
    lowest = h < HOP
    highest = h >= chain - HOP
    ahead = (c, lax.rem(h + 1, chain))
    behind = (c, lax.rem(h + chain - 1, chain))
    hop_ahead = (c, lax.rem(h + HOP, chain))
    hop_behind = (c, lax.rem(h + chain - HOP, chain))
    partner = (1 - c, h)
    cross_ahead = (1 - c, lax.rem(h + HOP, chain))
    cross_behind = (1 - c, lax.rem(h + chain - HOP, chain))

    def signal(semaphore, device):
        pl.semaphore_signal(semaphore, inc=1, device_id=device, device_id_type=mesh_id)

    barrier = pltpu.get_barrier_semaphore()
    signal(barrier, behind)
    signal(barrier, hop_behind)
    if pairs:
        signal(barrier, partner)

        @pl.when(lowest)
        def _():
            signal(barrier, cross_behind)

    @pl.when(h < last_link)
    def _():
        signal(barrier, ahead)

    @pl.when(jnp.logical_not(highest))
    def _():
        signal(barrier, hop_ahead)
        if pairs:
            signal(barrier, cross_ahead)

    fields = []
    for f in range(5):
        load = pltpu.make_async_copy(cons_hbm.at[f], cons.at[f], load_sems.at[4 + f])
        load.start()
        fields.append(load)
    loads = []
    for index, (source, target) in enumerate(
        ((links_hbm, links), (levels_hbm, levels), (deriv_hbm, deriv), (lift_hbm, lift))
    ):
        load = pltpu.make_async_copy(source, target, load_sems.at[index])
        load.start()
        loads.append(load)

    def remote(source, target, index, device):
        return pltpu.make_async_remote_copy(
            src_ref=source,
            dst_ref=target,
            send_sem=send_sems.at[index],
            recv_sem=recv_sems.at[index],
            device_id=device,
            device_id_type=mesh_id,
        )

    row = lax.broadcasted_iota(jnp.int32, (32, 64), 0)
    col = lax.broadcasted_iota(jnp.int32, (32, 64), 1)
    inside = lax.rem(row, 16)
    node = (inside // 4) * 16 + lax.rem(inside, 4) + jnp.where(row >= 16, 12, 0)
    picker = jnp.where(col == node, 1.0, 0.0).astype(jnp.bfloat16)

    for f in range(5):
        fields[f].wait()
        both = jnp.dot(picker, cons[f], preferred_element_type=jnp.float32)
        both = both.astype(jnp.bfloat16)
        own[2, f] = both[0:16]
        own[3, f] = both[16:32]

    copies = [
        remote(cons.at[:, 48:64, :], nb.at[0], 0, ahead),
        remote(cons.at[:, 0:16, :], nb.at[1], 1, behind),
        remote(own.at[3], nb.at[2], 2, hop_ahead),
    ]
    if pairs:
        ask = remote(asking, asked, 3, hop_ahead)
        serve = remote(serving.at[:, :, 0 : 3 * tile], served, 9, hop_behind)
        serve_cross = remote(serving.at[:, :, 3 * tile :], crossed, 10, cross_behind)
    else:
        copies.append(remote(own.at[2], nb.at[3], 3, hop_behind))
    loads[0].wait()
    asking[...] = links[3:4, :]
    expected = 6 if pairs else 4
    expected -= jnp.where(h == 0, 1, 0) + jnp.where(lowest, 2 if pairs else 1, 0)
    if pairs:
        expected += jnp.where(highest, 1, 0)
    pl.semaphore_wait(barrier, expected)

    if pairs:
        ask.start()

    @pl.when(h == last_link)
    def _():
        signal(ready_sems.at[0], ahead)
        copies[0].start()

    @pl.when(highest)
    def _():
        signal(ready_sems.at[1], hop_ahead)
        if pairs:
            signal(ready_sems.at[1], cross_ahead)
        copies[2].start()

    @pl.when(h < last_link)
    def _():
        copies[0].start()

    @pl.when(h > 0)
    def _():
        copies[1].start()

    @pl.when(jnp.logical_not(highest))
    def _():
        copies[2].start()

    if pairs:
        moved_copy = remote(cons.at[:, :, 3 * tile :], moved, 4, partner)
        level_copy = remote(levels.at[:, 3 * tile :], moved_levels, 5, partner)
        moved_copy.start()
        loads[1].wait()
        level_copy.start()
    else:
        loads[1].wait()

        @pl.when(jnp.logical_not(lowest))
        def _():
            copies[3].start()

    rows_step = 128
    lanes = lax.broadcasted_iota(jnp.int32, (rows_step, tile), 0)

    def columns(t):
        return pl.ds(pl.multiple_of(t * tile, tile), tile)

    def build_tile(face, link, cols):
        for r in range(0, slots, rows_step):
            hot[face, r : r + rows_step, cols] = jnp.where(
                lanes == link - r, 1.0, 0.0
            ).astype(jnp.bfloat16)

    def build(face):
        def step(t, carry):
            cols = columns(t)
            build_tile(face, links[face : face + 1, cols], cols)
            return carry

        lax.fori_loop(0, 4, step, 0)

    build(0)
    build(1)

    def wrap_behind():
        @pl.when(h == 0)
        def _():
            pl.semaphore_wait(ready_sems.at[0], 1)
            copies[1].start()

    if not pairs:
        wrap_behind()

        @pl.when(lowest)
        def _():
            pl.semaphore_wait(ready_sems.at[1], 1)
            copies[3].start()

    build(2)
    if not pairs:
        build(3)
    for f in range(5):
        own[0, f] = cons[f, 0:16, :]
        own[1, f] = cons[f, 48:64, :]
    loads[2].wait()
    loads[3].wait()

    operator = jnp.concatenate([deriv[0], deriv[1], deriv[2]], axis=1)

    def node_fluxes(w, n):
        inv, pressure = primitives(w)
        for d in range(3):
            pieces, _ = flux(w, inv, pressure, d)
            for f in range(5):
                fluxes[f, 64 * d + n : 64 * d + n + 16, :] = pieces[f].astype(jnp.bfloat16)

    def scale_of(block):
        return TIME_STEP * (jnp.int32(1) << block).astype(jnp.float32)

    def volume_step(t, carry):
        cols = columns(t)
        for n in range(0, 64, 16):
            node_fluxes([cons[f, n : n + 16, cols].astype(jnp.float32) for f in range(5)], n)
        factor = scale_of(levels[:, cols])
        for f in range(5):
            volume = jnp.dot(operator, fluxes[f], preferred_element_type=jnp.float32)
            pre[f, :, cols] = cons[f, :, cols].astype(jnp.float32) - factor * volume
        return carry

    def jump_tile(face, cols):
        source = nb[face].reshape(80, slots)
        picked = jnp.dot(source, hot[face, :, cols], preferred_element_type=jnp.float32)
        neighbour = [picked[16 * f : 16 * f + 16] for f in range(5)]
        inner = [own[face, f, :, cols].astype(jnp.float32) for f in range(5)]
        orient = jnp.where(lax.rem(face, 2) == 0, -1.0, 1.0)
        jumps = signed_jump(inner, neighbour, face < 2, orient)
        return [jump.astype(jnp.bfloat16) for jump in jumps]

    def face_rows(face):
        return pl.ds(pl.multiple_of(16 * face, 16), 16)

    def keep_jumps(face, count):
        def step(t, carry):
            cols = columns(t)
            jumps = jump_tile(face, cols)
            for f in range(5):
                jmp[f, face_rows(face), cols] = jumps[f]
            return carry

        lax.fori_loop(0, count, step, 0)

    def finish(cols):
        factor = scale_of(levels[:, cols])
        for f in range(5):
            surface = jnp.dot(lift[...], jmp[f, :, cols], preferred_element_type=jnp.float32)
            done[f, :, cols] = (pre[f, :, cols] + factor * surface).astype(jnp.bfloat16)

    def finish_step(t, carry):
        finish(columns(t))
        return carry

    def wait_face(face):
        remote(own.at[face], nb.at[face], face, partner).wait_recv()

    inner_face = jnp.where(lax.rem(h, 2) == 0, 1, 0)
    if not pairs:
        lax.fori_loop(0, 4, volume_step, 0)

        def whole_face(face, carry):
            wait_face(face)
            keep_jumps(face, 4)
            return carry

        lax.fori_loop(0, 4, whole_face, 0)
        lax.fori_loop(0, 4, finish_step, 0)
        out_levels[...] = levels[...]
        third_pre[...] = jnp.zeros_like(third_pre)
        third_jmp[...] = jnp.zeros_like(third_jmp)
        for copy in copies:
            copy.wait_send()
        return

    last = pl.ds(3 * tile, tile)
    third = pl.ds(2 * tile, tile)

    def choose(mine, other):
        full = jnp.broadcast_to(counts[0, 0], mine.shape) == slots
        chosen = jnp.where(full, mine.astype(jnp.float32), other.astype(jnp.float32))
        return chosen.astype(mine.dtype)

    def serve_tile(t, carry):
        cols = columns(t)
        build_tile(3, asked[:, cols], cols)
        source = own[2].reshape(80, slots)
        picked = jnp.dot(source, hot[3, :, cols], preferred_element_type=jnp.float32)
        for f in range(5):
            serving[f, :, cols] = picked[16 * f : 16 * f + 16].astype(jnp.bfloat16)
        return carry

    def answer():
        ask.wait_recv()
        serve_tile(jnp.int32(3), 0)

        @pl.when(lowest)
        def _():
            pl.semaphore_wait(ready_sems.at[1], 2)

        serve_cross.start()
        lax.fori_loop(0, 3, serve_tile, 0)
        serve.start()

    def jump_copy(face):
        return remote(leaving.at[face], arrived.at[face], 6 + face, partner)

    def lead(face):
        wait_face(face)
        jumps = jump_tile(face, last)
        for f in range(5):
            leaving[face, f] = jumps[f]
        jump_copy(face).start()

    def settle(face):
        jump_copy(face).wait_recv()
        for f in range(5):
            mine = jmp[f, face_rows(face), third]
            third_jmp[f, face_rows(face), :] = choose(mine, arrived[face, f])

    def served_jumps(inner, neighbour):
        inner = [u.astype(jnp.float32) for u in inner]
        neighbour = [w.astype(jnp.float32) for w in neighbour]
        jumps = face_jump(inner, neighbour, FACE_AXES[3], FACE_SIGNS[3])
        return [jump.astype(jnp.bfloat16) for jump in jumps]

    def served_step(t, carry):
        cols = columns(t)
        jumps = served_jumps(
            [own[3, f, :, cols] for f in range(5)], [served[f, :, cols] for f in range(5)]
        )
        for f in range(5):
            jmp[f, 48:64, cols] = jumps[f]
        return carry

    middle = jnp.logical_not(lowest | highest)
    outer_late = middle & (lax.rem(h, HOP) == HOP - 1)
    order = [
        inner_face,
        jnp.where(outer_late, 2, 1 - inner_face),
        jnp.where(outer_late, 1 - inner_face, 2),
    ]

    lax.fori_loop(0, 2, volume_step, 0)

    lead(order[0])
    keep_jumps(order[0], 3)
    wrap_behind()
    answer()

    out_levels[:, 0 : 2 * tile] = levels[:, 0 : 2 * tile]
    out_levels[:, last] = jnp.zeros((1, tile), jnp.int32)

    level_copy.wait_recv()
    full_row = jnp.broadcast_to(counts[0, 0], (1, tile)) == slots
    chosen_levels = jnp.where(full_row, levels[:, third], moved_levels[...])
    out_levels[:, third] = chosen_levels
    factor = scale_of(chosen_levels)
    moved_copy.wait_recv()
    for n in range(0, 64, 16):
        w = []
        for f in range(5):
            chosen = choose(cons[f, n : n + 16, third], moved[f, n : n + 16, :])
            w.append(chosen.astype(jnp.float32))
            third_pre[f, n : n + 16, :] = w[f]
        node_fluxes(w, n)
    for f in range(5):
        volume = jnp.dot(operator, fluxes[f], preferred_element_type=jnp.float32)
        third_pre[f] = third_pre[f] - factor * volume
        both = jnp.dot(picker, moved[f], preferred_element_type=jnp.float32)
        third_own[f] = choose(own[3, f, :, third], both[16:32].astype(jnp.bfloat16))

    lead(order[1])
    lead(order[2])
    keep_jumps(order[1], 3)
    keep_jumps(order[2], 3)
    settle(order[0])
    settle(order[1])
    serve.wait_recv()
    lax.fori_loop(0, 2, served_step, 0)
    lax.fori_loop(0, 2, finish_step, 0)
    serve_cross.wait_recv()
    beyond = [choose(served[f, :, third], crossed[f]) for f in range(5)]
    jumps = served_jumps([third_own[f] for f in range(5)], beyond)
    for f in range(5):
        third_jmp[f, 48:64, :] = jumps[f]
    settle(order[2])
    sent = copies + [ask, serve, serve_cross, moved_copy, level_copy]
    for copy in sent + [jump_copy(face) for face in range(3)]:
        copy.wait_send()


def write_kernel(done, levels, lift, pre, jmp, out, out_levels, fresh, blank, sems):
    tile = pre.shape[-1]
    copies = [
        pltpu.make_async_copy(done, out.at[:, :, 0 : 2 * tile], sems.at[0]),
        pltpu.make_async_copy(levels, out_levels, sems.at[1]),
        pltpu.make_async_copy(blank, out.at[:, :, 3 * tile :], sems.at[2]),
    ]
    copies[0].start()
    copies[1].start()
    factor = TIME_STEP * (jnp.int32(1) << levels[:, 2 * tile : 3 * tile]).astype(jnp.float32)
    for f in range(5):
        surface = jnp.dot(lift[...], jmp[f], preferred_element_type=jnp.float32)
        fresh[f] = (pre[f] + factor * surface).astype(jnp.bfloat16)
        copy = pltpu.make_async_copy(
            fresh.at[f], out.at[f, :, 2 * tile : 3 * tile], sems.at[3 + f]
        )
        copy.start()
        copies.append(copy)
    blank[...] = jnp.zeros_like(blank)
    copies[2].start()
    for copy in copies:
        copy.wait()


def stay(block):
    return pltpu.with_memory_space_constraint(block, pltpu.HBM)


def per_device(conserved, element_counts, face_links, refinement, derivative, face_lift):
    slots = conserved.shape[-1]
    tile = slots // 4
    pairs = lax.axis_size("cube") == 2
    vmem = pl.BlockSpec(memory_space=pltpu.VMEM)
    hbm = pl.BlockSpec(memory_space=pltpu.HBM)
    smem = pl.BlockSpec(memory_space=pltpu.SMEM)
    half = jnp.bfloat16
    kept = 2 * tile if pairs else slots
    parts = pl.pallas_call(
        functools.partial(section_kernel, pairs, lax.axis_size("chain")),
        out_shape=(
            jax.ShapeDtypeStruct((5, 64, kept), half),
            jax.ShapeDtypeStruct((1, slots), jnp.int32),
            jax.ShapeDtypeStruct((64, 64), half),
            jax.ShapeDtypeStruct((5, 64, tile), jnp.float32),
            jax.ShapeDtypeStruct((5, 64, tile), half),
        ),
        in_specs=[hbm, hbm, hbm, smem, hbm, hbm],
        out_specs=(vmem,) * 5,
        scratch_shapes=[
            pltpu.VMEM((5, 64, slots), half),
            pltpu.VMEM((4, slots), jnp.int32),
            pltpu.VMEM((1, slots), jnp.int32),
            pltpu.VMEM((3, 64, 64), half),
            pltpu.VMEM((4, 5, 16, slots), half),
            pltpu.VMEM((4, 5, 16, slots), half),
            pltpu.VMEM((4, slots, slots), half),
            pltpu.VMEM((5, 192, tile), half),
            pltpu.VMEM((5, 64, slots), jnp.float32),
            pltpu.VMEM((5, 64, slots), half),
            pltpu.VMEM((5, 64, tile), half),
            pltpu.VMEM((1, tile), jnp.int32),
            pltpu.VMEM((3, 5, 16, tile), half),
            pltpu.VMEM((3, 5, 16, tile), half),
            pltpu.VMEM((1, slots), jnp.int32),
            pltpu.VMEM((1, slots), jnp.int32),
            pltpu.VMEM((5, 16, slots), half),
            pltpu.VMEM((5, 16, 3 * tile), half),
            pltpu.VMEM((5, 16, tile), half),
            pltpu.VMEM((5, 16, tile), half),
            pltpu.SemaphoreType.DMA((9,)),
            pltpu.SemaphoreType.DMA((11,)),
            pltpu.SemaphoreType.DMA((11,)),
            pltpu.SemaphoreType.REGULAR((2,)),
        ],
        compiler_params=pltpu.CompilerParams(
            collective_id=0, has_side_effects=True, vmem_limit_bytes=40 << 20
        ),
    )(
        stay(conserved[0, 0]),
        stay(face_links[0, 0]),
        stay(refinement[0]),
        element_counts,
        stay(derivative),
        stay(face_lift),
    )
    if pairs:
        fresh, levels = pl.pallas_call(
            write_kernel,
            out_shape=(
                jax.ShapeDtypeStruct((5, 64, slots), half),
                jax.ShapeDtypeStruct((1, slots), jnp.int32),
            ),
            in_specs=[vmem] * 5,
            out_specs=(hbm, hbm),
            scratch_shapes=[
                pltpu.VMEM((5, 64, tile), half),
                pltpu.VMEM((5, 64, tile), half),
                pltpu.SemaphoreType.DMA((8,)),
            ],
            compiler_params=pltpu.CompilerParams(vmem_limit_bytes=8 << 20),
        )(*parts)
    else:
        fresh, moved, _ = migrate(
            parts[0], parts[1][0].astype(jnp.bfloat16), element_counts[0, 0]
        )
        levels = moved.astype(jnp.int32)[None]
    return (fresh[None, None], levels[None])


def solution(mesh):
    placed = (
        P("cube", "chain", None, None, None),
        P("cube", "chain"),
        P("cube", "chain", None, None),
        P("cube", "chain", None),
        P(),
        P(),
    )
    return jax.shard_map(
        per_device,
        mesh=mesh,
        in_specs=placed,
        out_specs=(P("cube", "chain", None, None, None), P("cube", "chain", None)),
        check_vma=False,
    )
```

```python
import functools

import jax
import jax.numpy as jnp
from jax import lax
from jax.experimental import pallas as pl
from jax.experimental.pallas import tpu as pltpu
from jax.sharding import PartitionSpec as P

HOP = 4


HEAT_RATIO = 1.4
TIME_STEP = 0.08
FACE_AXES = (2, 2, 1, 1)
FACE_SIGNS = (-1.0, 1.0, -1.0, 1.0)


def from_partner(block, axis, distance):
    count = lax.axis_size(axis)
    route = []
    for low in range(count):
        high = low | 1 << distance
        if high != low and high < count:
            route += [(low, high), (high, low)]
    return lax.ppermute(block, axis, route)


def send_window(values, staying, capacity):
    slot_count = values.shape[-1]
    start = jnp.minimum(staying, slot_count - capacity)
    return lax.dynamic_slice_in_dim(values, start, capacity, axis=values.ndim - 1)


def land_window(values, received, keep, arriving, partner_staying, capacity):
    slot_axis = values.ndim - 1
    slot_count = values.shape[-1]
    shift = partner_staying - jnp.minimum(partner_staying, slot_count - capacity)
    target = jnp.minimum(keep, slot_count - capacity)
    zero_rows = jnp.zeros(received.shape[:-1] + (capacity,), received.dtype)
    padded = jnp.concatenate([zero_rows, received, zero_rows], axis=slot_axis)
    aligned = lax.dynamic_slice_in_dim(
        padded, capacity + shift - (keep - target), capacity, axis=slot_axis
    )
    position = jnp.arange(slot_count, dtype=jnp.int32)
    kept = jnp.where(position < keep, values, jnp.zeros_like(values))
    region = lax.dynamic_slice_in_dim(kept, target, capacity, axis=slot_axis)
    slot_here = target + jnp.arange(capacity, dtype=jnp.int32)
    update = jnp.where((slot_here >= keep) & (slot_here < keep + arriving), aligned, region)
    return lax.dynamic_update_slice_in_dim(kept, update, target, axis=slot_axis)


def migrate(values, levels, current):
    slot_count = values.shape[-1]
    capacity = slot_count // 4
    rounds_count = lax.axis_size("cube").bit_length() - 1
    for exponent in range(rounds_count):
        partner = from_partner(jnp.reshape(current, (1,)), "cube", exponent)[0]
        leaving = jnp.maximum(current - partner, 0) // 2
        arriving = jnp.maximum(partner - current, 0) // 2
        staying = current - leaving
        partner_staying = partner - arriving
        out_values = send_window(values, staying, capacity)
        out_levels = send_window(levels, staying, capacity)
        in_values, in_levels = from_partner((out_values, out_levels), "cube", exponent)
        values = land_window(values, in_values, staying, arriving, partner_staying, capacity)
        levels = land_window(levels, in_levels, staying, arriving, partner_staying, capacity)
        current = staying + arriving
    return (values, levels, current)


def primitives(w):
    inv = 1.0 / w[0]
    kinetic = w[1] * w[1] + w[2] * w[2] + w[3] * w[3]
    pressure = (HEAT_RATIO - 1.0) * (w[4] - 0.5 * kinetic * inv)
    return inv, pressure


def flux(w, inv, pressure, axis_id):
    momentum = w[1 + axis_id]
    velocity = momentum * inv
    pieces = [momentum]
    for column in range(3):
        component = w[1 + column] * velocity
        if column == axis_id:
            component = component + pressure
        pieces.append(component)
    pieces.append((w[4] + pressure) * velocity)
    return pieces, velocity


def face_jump(inner, neighbour, axis_id, orient):
    inner_inv, inner_press = primitives(inner)
    outer_inv, outer_press = primitives(neighbour)
    inner_flux, inner_vel = flux(inner, inner_inv, inner_press, axis_id)
    outer_flux, outer_vel = flux(neighbour, outer_inv, outer_press, axis_id)
    half_speed = 0.5 * jnp.maximum(
        jnp.abs(inner_vel) + jnp.sqrt(HEAT_RATIO * inner_press * inner_inv),
        jnp.abs(outer_vel) + jnp.sqrt(HEAT_RATIO * outer_press * outer_inv),
    )
    return [
        (0.5 * orient) * (inner_flux[f] - outer_flux[f]) + half_speed * (neighbour[f] - inner[f])
        for f in range(5)
    ]


def signed_jump(inner, neighbour, vertical, orient):
    def side(w):
        inv, pressure = primitives(w)
        momentum = jnp.where(vertical, w[3], w[2])
        velocity = momentum * inv
        along_y = jnp.where(vertical, 0.0, pressure)
        along_z = jnp.where(vertical, pressure, 0.0)
        pieces = [
            momentum,
            w[1] * velocity,
            w[2] * velocity + along_y,
            w[3] * velocity + along_z,
            (w[4] + pressure) * velocity,
        ]
        return pieces, jnp.abs(velocity) + jnp.sqrt(HEAT_RATIO * pressure * inv)

    inner_flux, inner_speed = side(inner)
    outer_flux, outer_speed = side(neighbour)
    half_speed = 0.5 * jnp.maximum(inner_speed, outer_speed)
    half_sign = 0.5 * orient
    return [
        half_sign * (inner_flux[f] - outer_flux[f]) + half_speed * (neighbour[f] - inner[f])
        for f in range(5)
    ]


def section_kernel(
    pairs,
    chain,
    cons_hbm,
    links_hbm,
    levels_hbm,
    counts,
    deriv_hbm,
    lift_hbm,
    done,
    out_levels,
    lift,
    third_pre,
    third_jmp,
    cons,
    links,
    levels,
    deriv,
    own,
    nb,
    hot,
    fluxes,
    pre,
    jmp,
    moved,
    moved_levels,
    leaving,
    arrived,
    asking,
    asked,
    serving,
    served,
    crossed,
    merged,
    third_own,
    load_sems,
    send_sems,
    recv_sems,
    ready_sems,
):
    slots = cons.shape[-1]
    tile = slots // 4
    mesh_id = pl.DeviceIdType.MESH
    c = lax.axis_index("cube")
    h = lax.axis_index("chain")
    last_link = chain - 1
    lowest = h < HOP
    highest = h >= chain - HOP
    ahead = (c, lax.rem(h + 1, chain))
    behind = (c, lax.rem(h + chain - 1, chain))
    hop_ahead = (c, lax.rem(h + HOP, chain))
    hop_behind = (c, lax.rem(h + chain - HOP, chain))
    partner = (1 - c, h)

    def signal(semaphore, device):
        pl.semaphore_signal(semaphore, inc=1, device_id=device, device_id_type=mesh_id)

    barrier = pltpu.get_barrier_semaphore()
    signal(barrier, behind)
    signal(barrier, hop_behind)
    if pairs:
        signal(barrier, partner)

    @pl.when(h < last_link)
    def _():
        signal(barrier, ahead)

    @pl.when(jnp.logical_not(highest))
    def _():
        signal(barrier, hop_ahead)

    fields = []
    for f in range(5):
        load = pltpu.make_async_copy(cons_hbm.at[f], cons.at[f], load_sems.at[4 + f])
        load.start()
        fields.append(load)
    loads = []
    for index, (source, target) in enumerate(
        ((links_hbm, links), (levels_hbm, levels), (deriv_hbm, deriv), (lift_hbm, lift))
    ):
        load = pltpu.make_async_copy(source, target, load_sems.at[index])
        load.start()
        loads.append(load)

    def remote(source, target, index, device):
        return pltpu.make_async_remote_copy(
            src_ref=source,
            dst_ref=target,
            send_sem=send_sems.at[index],
            recv_sem=recv_sems.at[index],
            device_id=device,
            device_id_type=mesh_id,
        )

    row = lax.broadcasted_iota(jnp.int32, (32, 64), 0)
    col = lax.broadcasted_iota(jnp.int32, (32, 64), 1)
    inside = lax.rem(row, 16)
    node = (inside // 4) * 16 + lax.rem(inside, 4) + jnp.where(row >= 16, 12, 0)
    picker = jnp.where(col == node, 1.0, 0.0).astype(jnp.bfloat16)

    expected = 5 if pairs else 4
    expected -= jnp.where(h == 0, 1, 0) + jnp.where(lowest, 1, 0)

    @pl.when(h == last_link)
    def _():
        pl.semaphore_wait(barrier, expected)
        signal(ready_sems.at[0], ahead)
        remote(cons_hbm.at[:, 48:64, :], nb.at[0], 0, ahead).start()

    for f in range(5):
        fields[f].wait()
        both = jnp.dot(picker, cons[f], preferred_element_type=jnp.float32)
        both = both.astype(jnp.bfloat16)
        own[2, f] = both[0:16]
        own[3, f] = both[16:32]

    copies = [
        remote(cons.at[:, 48:64, :], nb.at[0], 0, ahead),
        remote(cons.at[:, 0:16, :], nb.at[1], 1, behind),
        remote(own.at[3], nb.at[2], 2, hop_ahead),
    ]
    if pairs:
        ask = remote(asking, asked, 3, hop_ahead)
        serve = remote(serving.at[:, :, 0 : 2 * tile], served.at[:, :, 0 : 2 * tile], 9, hop_behind)
        trade = remote(serving.at[:, :, 3 * tile :], crossed, 10, partner)
        serve_third = remote(merged, served.at[:, :, 2 * tile :], 11, hop_behind)
    else:
        copies.append(remote(own.at[2], nb.at[3], 3, hop_behind))
    loads[0].wait()
    full_mark = jnp.where(jnp.broadcast_to(counts[0, 0], (1, slots)) == slots, 2 * slots, 0)
    asking[...] = links[3:4, :] + full_mark
    @pl.when(h < last_link)
    def _():
        pl.semaphore_wait(barrier, expected)

    if pairs:
        ask.start()

    @pl.when(highest)
    def _():
        signal(ready_sems.at[1], hop_ahead)
        copies[2].start()

    @pl.when(h < last_link)
    def _():
        copies[0].start()

    @pl.when(h > 0)
    def _():
        copies[1].start()

    @pl.when(jnp.logical_not(highest))
    def _():
        copies[2].start()

    if pairs:
        moved_copy = remote(cons.at[:, :, 3 * tile :], moved, 4, partner)
        level_copy = remote(levels.at[:, 3 * tile :], moved_levels, 5, partner)
        moved_copy.start()
        loads[1].wait()
        level_copy.start()
    else:
        loads[1].wait()

        @pl.when(jnp.logical_not(lowest))
        def _():
            copies[3].start()

    rows_step = 128
    lanes = lax.broadcasted_iota(jnp.int32, (rows_step, tile), 0)

    def columns(t):
        return pl.ds(pl.multiple_of(t * tile, tile), tile)

    def build_tile(face, link, cols):
        for r in range(0, slots, rows_step):
            hot[face, r : r + rows_step, cols] = jnp.where(
                lanes == link - r, 1.0, 0.0
            ).astype(jnp.bfloat16)

    def build(face):
        def step(t, carry):
            cols = columns(t)
            build_tile(face, links[face : face + 1, cols], cols)
            return carry

        lax.fori_loop(0, 4, step, 0)

    build(0)
    build(1)

    def wrap_behind():
        @pl.when(h == 0)
        def _():
            pl.semaphore_wait(ready_sems.at[0], 1)
            copies[1].start()

    if not pairs:
        wrap_behind()

        @pl.when(lowest)
        def _():
            pl.semaphore_wait(ready_sems.at[1], 1)
            copies[3].start()

    build(2)
    if not pairs:
        build(3)
    for f in range(5):
        own[0, f] = cons[f, 0:16, :]
        own[1, f] = cons[f, 48:64, :]
    loads[2].wait()
    loads[3].wait()

    operator = jnp.concatenate([deriv[0], deriv[1], deriv[2]], axis=1)

    def node_fluxes(w, n):
        inv, pressure = primitives(w)
        for d in range(3):
            pieces, _ = flux(w, inv, pressure, d)
            for f in range(5):
                fluxes[f, 64 * d + n : 64 * d + n + 16, :] = pieces[f].astype(jnp.bfloat16)

    def scale_of(block):
        return TIME_STEP * (jnp.int32(1) << block).astype(jnp.float32)

    def volume_step(t, carry):
        cols = columns(t)
        for n in range(0, 64, 16):
            node_fluxes([cons[f, n : n + 16, cols].astype(jnp.float32) for f in range(5)], n)
        factor = scale_of(levels[:, cols])
        for f in range(5):
            volume = jnp.dot(operator, fluxes[f], preferred_element_type=jnp.float32)
            pre[f, :, cols] = cons[f, :, cols].astype(jnp.float32) - factor * volume
        return carry

    def jump_tile(face, cols):
        source = nb[face].reshape(80, slots)
        picked = jnp.dot(source, hot[face, :, cols], preferred_element_type=jnp.float32)
        neighbour = [picked[16 * f : 16 * f + 16] for f in range(5)]
        inner = [own[face, f, :, cols].astype(jnp.float32) for f in range(5)]
        orient = jnp.where(lax.rem(face, 2) == 0, -1.0, 1.0)
        jumps = signed_jump(inner, neighbour, face < 2, orient)
        return [jump.astype(jnp.bfloat16) for jump in jumps]

    def face_rows(face):
        return pl.ds(pl.multiple_of(16 * face, 16), 16)

    def keep_jumps(face, count):
        def step(t, carry):
            cols = columns(t)
            jumps = jump_tile(face, cols)
            for f in range(5):
                jmp[f, face_rows(face), cols] = jumps[f]
            return carry

        lax.fori_loop(0, count, step, 0)

    def finish(cols):
        factor = scale_of(levels[:, cols])
        for f in range(5):
            surface = jnp.dot(lift[...], jmp[f, :, cols], preferred_element_type=jnp.float32)
            done[f, :, cols] = (pre[f, :, cols] + factor * surface).astype(jnp.bfloat16)

    def finish_step(t, carry):
        finish(columns(t))
        return carry

    def wait_face(face):
        remote(own.at[face], nb.at[face], face, partner).wait_recv()

    inner_face = jnp.where(lax.rem(h, 2) == 0, 1, 0)
    if not pairs:
        lax.fori_loop(0, 4, volume_step, 0)

        def whole_face(face, carry):
            wait_face(face)
            keep_jumps(face, 4)
            return carry

        lax.fori_loop(0, 4, whole_face, 0)
        lax.fori_loop(0, 4, finish_step, 0)
        out_levels[...] = levels[...]
        third_pre[...] = jnp.zeros_like(third_pre)
        third_jmp[...] = jnp.zeros_like(third_jmp)
        for copy in copies:
            copy.wait_send()
        return

    last = pl.ds(3 * tile, tile)
    third = pl.ds(2 * tile, tile)

    def choose(mine, other):
        full = jnp.broadcast_to(counts[0, 0], mine.shape) == slots
        chosen = jnp.where(full, mine.astype(jnp.float32), other.astype(jnp.float32))
        return chosen.astype(mine.dtype)

    def serve_tile(t, carry):
        cols = columns(t)
        link = asked[:, cols]
        build_tile(3, jnp.where(link >= 2 * slots, link - 2 * slots, link), cols)
        source = own[2].reshape(80, slots)
        picked = jnp.dot(source, hot[3, :, cols], preferred_element_type=jnp.float32)
        for f in range(5):
            serving[f, :, cols] = picked[16 * f : 16 * f + 16].astype(jnp.bfloat16)
        return carry

    def answer():
        ask.wait_recv()
        serve_tile(jnp.int32(3), 0)

        trade.start()
        lax.fori_loop(0, 2, serve_tile, 0)

        @pl.when(lowest)
        def _():
            pl.semaphore_wait(ready_sems.at[1], 1)

        serve.start()
        serve_tile(jnp.int32(2), 0)

    def answer_third():
        trade.wait_recv()
        full = asked[:, 2 * tile : 3 * tile] >= 2 * slots
        for f in range(5):
            mine = serving[f, :, 2 * tile : 3 * tile].astype(jnp.float32)
            other = crossed[f].astype(jnp.float32)
            merged[f] = jnp.where(full, mine, other).astype(jnp.bfloat16)
        serve_third.start()

    def jump_copy(face):
        return remote(leaving.at[face], arrived.at[face], 6 + face, partner)

    def lead(face):
        wait_face(face)
        jumps = jump_tile(face, last)
        for f in range(5):
            leaving[face, f] = jumps[f]
        jump_copy(face).start()

    def settle(face):
        jump_copy(face).wait_recv()
        for f in range(5):
            mine = jmp[f, face_rows(face), third]
            third_jmp[f, face_rows(face), :] = choose(mine, arrived[face, f])

    def served_jumps(inner, neighbour):
        inner = [u.astype(jnp.float32) for u in inner]
        neighbour = [w.astype(jnp.float32) for w in neighbour]
        jumps = face_jump(inner, neighbour, FACE_AXES[3], FACE_SIGNS[3])
        return [jump.astype(jnp.bfloat16) for jump in jumps]

    def served_step(t, carry):
        cols = columns(t)
        jumps = served_jumps(
            [own[3, f, :, cols] for f in range(5)], [served[f, :, cols] for f in range(5)]
        )
        for f in range(5):
            jmp[f, 48:64, cols] = jumps[f]
        return carry

    middle = jnp.logical_not(lowest | highest)
    outer_late = middle & (lax.rem(h, HOP) == HOP - 1)
    order = [
        inner_face,
        jnp.where(outer_late, 2, 1 - inner_face),
        jnp.where(outer_late, 1 - inner_face, 2),
    ]

    lax.fori_loop(0, 2, volume_step, 0)

    lead(order[0])
    keep_jumps(order[0], 3)
    wrap_behind()
    answer()

    out_levels[:, 0 : 2 * tile] = levels[:, 0 : 2 * tile]
    out_levels[:, last] = jnp.zeros((1, tile), jnp.int32)

    level_copy.wait_recv()
    full_row = jnp.broadcast_to(counts[0, 0], (1, tile)) == slots
    chosen_levels = jnp.where(full_row, levels[:, third], moved_levels[...])
    out_levels[:, third] = chosen_levels
    factor = scale_of(chosen_levels)
    moved_copy.wait_recv()
    for n in range(0, 64, 16):
        w = []
        for f in range(5):
            chosen = choose(cons[f, n : n + 16, third], moved[f, n : n + 16, :])
            w.append(chosen.astype(jnp.float32))
            third_pre[f, n : n + 16, :] = w[f]
        node_fluxes(w, n)
    for f in range(5):
        volume = jnp.dot(operator, fluxes[f], preferred_element_type=jnp.float32)
        third_pre[f] = third_pre[f] - factor * volume
        both = jnp.dot(picker, moved[f], preferred_element_type=jnp.float32)
        third_own[f] = choose(own[3, f, :, third], both[16:32].astype(jnp.bfloat16))

    @pl.when(jnp.logical_not(lowest))
    def _():
        answer_third()

    lead(order[1])
    lead(order[2])

    @pl.when(lowest)
    def _():
        answer_third()

    keep_jumps(order[1], 3)
    keep_jumps(order[2], 3)
    settle(order[0])
    serve.wait_recv()
    lax.fori_loop(0, 2, served_step, 0)
    lax.fori_loop(0, 2, finish_step, 0)
    serve_third.wait_recv()
    jumps = served_jumps(
        [third_own[f] for f in range(5)], [served[f, :, third] for f in range(5)]
    )
    for f in range(5):
        third_jmp[f, 48:64, :] = jumps[f]
    settle(order[1])
    settle(order[2])
    sent = copies + [ask, serve, trade, serve_third, moved_copy, level_copy]
    for copy in sent + [jump_copy(face) for face in range(3)]:
        copy.wait_send()


def write_kernel(done, levels, lift, pre, jmp, out, out_levels, fresh, blank, sems):
    tile = pre.shape[-1]
    copies = [
        pltpu.make_async_copy(done, out.at[:, :, 0 : 2 * tile], sems.at[0]),
        pltpu.make_async_copy(levels, out_levels, sems.at[1]),
        pltpu.make_async_copy(blank, out.at[:, :, 3 * tile :], sems.at[2]),
    ]
    copies[0].start()
    copies[1].start()
    factor = TIME_STEP * (jnp.int32(1) << levels[:, 2 * tile : 3 * tile]).astype(jnp.float32)
    for f in range(5):
        surface = jnp.dot(lift[...], jmp[f], preferred_element_type=jnp.float32)
        fresh[f] = (pre[f] + factor * surface).astype(jnp.bfloat16)
        copy = pltpu.make_async_copy(
            fresh.at[f], out.at[f, :, 2 * tile : 3 * tile], sems.at[3 + f]
        )
        copy.start()
        copies.append(copy)
    blank[...] = jnp.zeros_like(blank)
    copies[2].start()
    for copy in copies:
        copy.wait()


def stay(block):
    return pltpu.with_memory_space_constraint(block, pltpu.HBM)


def per_device(conserved, element_counts, face_links, refinement, derivative, face_lift):
    slots = conserved.shape[-1]
    tile = slots // 4
    pairs = lax.axis_size("cube") == 2
    vmem = pl.BlockSpec(memory_space=pltpu.VMEM)
    hbm = pl.BlockSpec(memory_space=pltpu.HBM)
    smem = pl.BlockSpec(memory_space=pltpu.SMEM)
    half = jnp.bfloat16
    kept = 2 * tile if pairs else slots
    parts = pl.pallas_call(
        functools.partial(section_kernel, pairs, lax.axis_size("chain")),
        out_shape=(
            jax.ShapeDtypeStruct((5, 64, kept), half),
            jax.ShapeDtypeStruct((1, slots), jnp.int32),
            jax.ShapeDtypeStruct((64, 64), half),
            jax.ShapeDtypeStruct((5, 64, tile), jnp.float32),
            jax.ShapeDtypeStruct((5, 64, tile), half),
        ),
        in_specs=[hbm, hbm, hbm, smem, hbm, hbm],
        out_specs=(vmem,) * 5,
        scratch_shapes=[
            pltpu.VMEM((5, 64, slots), half),
            pltpu.VMEM((4, slots), jnp.int32),
            pltpu.VMEM((1, slots), jnp.int32),
            pltpu.VMEM((3, 64, 64), half),
            pltpu.VMEM((4, 5, 16, slots), half),
            pltpu.VMEM((4, 5, 16, slots), half),
            pltpu.VMEM((4, slots, slots), half),
            pltpu.VMEM((5, 192, tile), half),
            pltpu.VMEM((5, 64, slots), jnp.float32),
            pltpu.VMEM((5, 64, slots), half),
            pltpu.VMEM((5, 64, tile), half),
            pltpu.VMEM((1, tile), jnp.int32),
            pltpu.VMEM((3, 5, 16, tile), half),
            pltpu.VMEM((3, 5, 16, tile), half),
            pltpu.VMEM((1, slots), jnp.int32),
            pltpu.VMEM((1, slots), jnp.int32),
            pltpu.VMEM((5, 16, slots), half),
            pltpu.VMEM((5, 16, 3 * tile), half),
            pltpu.VMEM((5, 16, tile), half),
            pltpu.VMEM((5, 16, tile), half),
            pltpu.VMEM((5, 16, tile), half),
            pltpu.SemaphoreType.DMA((9,)),
            pltpu.SemaphoreType.DMA((12,)),
            pltpu.SemaphoreType.DMA((12,)),
            pltpu.SemaphoreType.REGULAR((2,)),
        ],
        compiler_params=pltpu.CompilerParams(
            collective_id=0, has_side_effects=True, vmem_limit_bytes=40 << 20
        ),
    )(
        stay(conserved[0, 0]),
        stay(face_links[0, 0]),
        stay(refinement[0]),
        element_counts,
        stay(derivative),
        stay(face_lift),
    )
    if pairs:
        fresh, levels = pl.pallas_call(
            write_kernel,
            out_shape=(
                jax.ShapeDtypeStruct((5, 64, slots), half),
                jax.ShapeDtypeStruct((1, slots), jnp.int32),
            ),
            in_specs=[vmem] * 5,
            out_specs=(hbm, hbm),
            scratch_shapes=[
                pltpu.VMEM((5, 64, tile), half),
                pltpu.VMEM((5, 64, tile), half),
                pltpu.SemaphoreType.DMA((8,)),
            ],
            compiler_params=pltpu.CompilerParams(vmem_limit_bytes=8 << 20),
        )(*parts)
    else:
        fresh, moved, _ = migrate(
            parts[0], parts[1][0].astype(jnp.bfloat16), element_counts[0, 0]
        )
        levels = moved.astype(jnp.int32)[None]
    return (fresh[None, None], levels[None])


def solution(mesh):
    placed = (
        P("cube", "chain", None, None, None),
        P("cube", "chain"),
        P("cube", "chain", None, None),
        P("cube", "chain", None),
        P(),
        P(),
    )
    return jax.shard_map(
        per_device,
        mesh=mesh,
        in_specs=placed,
        out_specs=(P("cube", "chain", None, None, None), P("cube", "chain", None)),
        check_vma=False,
    )
```
